32 devices in a mesh: dp: 2 (over x), seq: 16 (over z, y, core).
Axes of the slice: x: 2, y: 2, z: 4, core: 2. Of those that a mesh axis runs over, the one named last changes fastest.
Arguments:
- query: bfloat16 [2048, 3072], P('seq', 'dp'), may hold values from -300 to 300
- key: bfloat16 [2048, 3072], P('seq', 'dp'), may hold values from -10 to 10
- value: bfloat16 [2048, 3072], P('seq', 'dp'), may hold values from -6 to 6
- d_query: bfloat16 [2048, 3072], P('seq', 'dp'), may hold values from -6 to 6
- d_key: bfloat16 [2048, 3072], P('seq', 'dp'), may hold values from -6 to 6
- d_value: bfloat16 [2048, 3072], P('seq', 'dp'), may hold values from -6 to 6
- residual: bfloat16 [2048, 3072], P('seq', 'dp'), may hold values from -6 to 6
- d_residual: bfloat16 [2048, 3072], P('seq', 'dp'), may hold values from -6 to 6
- w_in: bfloat16 [3072, 7168], P('seq', 'dp'), may hold values from -0.109375 to 0.109375
- w_out: bfloat16 [7168, 3072], P(('dp', 'seq')), may hold values from -0.125 to 0.125
Outputs:
- block_out: bfloat16 [2048, 3072], P('seq', 'dp')
- d_block_out: bfloat16 [2048, 3072], P('seq', 'dp')
The draws below stay inside these ranges and needn't reach their ends.
All inputs are finite; a program needn't handle non-finite values.
Results may differ from the reference program's by a relative error of at most 0.025.
Values may be sent and summed in bfloat16 or wider, within the bound.
A program may use at most 192 MiB of HBM per device.

```python
import jax
import jax.numpy as jnp
from jax import lax

HEAD_DIM = 128
HEADS = 24
D = 3072
FF = 7168
LENGTH = 2048


def joint_draw(base_key):
    folded = jax.random.fold_in(base_key, 11)
    key_a, key_b = jax.random.split(folded, 2)
    keys_arr = jnp.clip(jax.random.normal(key_a, (LENGTH, D), jnp.float32), -5.0, 5.0)
    queries = jnp.clip(jax.random.normal(key_b, (LENGTH, D), jnp.float32), -5.0, 5.0)
    return (queries, keys_arr)


def draw_query(base_key, part):
    return joint_draw(base_key)[0].astype(jnp.bfloat16)


def draw_key(base_key, part):
    return joint_draw(base_key)[1].astype(jnp.bfloat16)


def raised(values, key, source, target, parts, factor):
    owner, partner = [(jnp.arange(values.shape[position]) // (values.shape[position] // parts)).reshape([-1 if axis == position else 1 for axis in range(values.ndim)]) for position in (source, target)]
    chosen = jax.random.permutation(key, parts)[partner]
    strong = (owner == chosen) | (owner == (partner + parts // 2) % parts)
    return jnp.where(strong, factor * values, values)


def shard_levels(rng, shape, cuts, low, top_value):
    loudness = 1.0
    for position, blocks in cuts:
        draws = jax.random.uniform(jax.random.fold_in(jax.random.fold_in(rng, 6), position), (blocks,), jnp.float32, low / len(cuts), top_value / len(cuts))
        loudness = loudness * jnp.repeat(jnp.exp(draws), shape[position] // blocks).reshape((-1,) + (1,) * (len(shape) - 1 - position))
    return loudness


def scatter_about(rng, shape, deviation, bound, pieces=(), dtype=jnp.bfloat16):
    entries = deviation * jax.random.normal(rng, shape, jnp.float32)
    if pieces:
        entries = entries * shard_levels(rng, shape, pieces, -0.22, 0.18)
    return jnp.clip(entries, -bound, bound).astype(dtype)


def heavy_noise(rng, extent, spread, bound, pieces, heavy, held_as=jnp.bfloat16):
    result = spread * jax.random.normal(rng, extent, jnp.float32)
    if pieces:
        result = result * shard_levels(rng, extent, pieces, -0.22, 0.18)
    return jnp.clip(raised(result, jax.random.fold_in(rng, 3), *heavy), -bound, bound).astype(held_as)


def setup_inputs(seed: int = 0) -> dict:
    keys = jax.random.split(jax.random.key(seed), 11)
    query = draw_query(jax.random.fold_in(keys[10], 71), 0)
    key = draw_key(jax.random.fold_in(keys[10], 71), 0)
    value = scatter_about(keys[2], (LENGTH, D), 1.0, 6.0, ((0, 16), (1, 2)))
    d_query = scatter_about(keys[3], (LENGTH, D), 1.0, 6.0, ((0, 16), (1, 2)))
    d_key = scatter_about(keys[4], (LENGTH, D), 1.0, 6.0, ((0, 16), (1, 2)))
    d_value = scatter_about(keys[5], (LENGTH, D), 1.0, 6.0, ((0, 16), (1, 2)))
    residual = scatter_about(keys[6], (LENGTH, D), 1.0, 6.0, ((0, 16), (1, 2)))
    d_residual = scatter_about(keys[7], (LENGTH, D), 1.0, 6.0, ((0, 16), (1, 2)))
    w_in = scatter_about(keys[8], (D, FF), D ** -0.5, 0.109375, ((0, 16), (1, 2)))
    w_out = heavy_noise(keys[9], (FF, D), FF ** -0.5, 0.125, ((0, 32),), (0, 1, 32, 2.75))
    return dict(query=query, key=key, value=value, d_query=d_query, d_key=d_key, d_value=d_value, residual=residual, d_residual=d_residual, w_in=w_in, w_out=w_out)


gelu_coeff = 0.7978845608
cubic_coeff = 0.044715

def gelu_pair(pre_act, d_pre_act):
    inner_arg = gelu_coeff * (pre_act + cubic_coeff * pre_act * pre_act * pre_act)
    hyper = jnp.tanh(inner_arg)
    gelu_value = 0.5 * pre_act * (1.0 + hyper)
    gelu_slope = 0.5 * (1.0 + hyper) + 0.5 * pre_act * (1.0 - hyper * hyper) * gelu_coeff * (1.0 + 3.0 * cubic_coeff * pre_act * pre_act)
    return (gelu_value, gelu_slope * d_pre_act)

def head_attend(operands):
    query_head, key_head, value_head, dquery_head, dkey_head, dvalue_head = operands
    score_scale = 1.0 / jnp.sqrt(jnp.float32(HEAD_DIM))
    scores = jnp.dot(query_head, key_head.T, preferred_element_type=jnp.float32) * score_scale
    d_scores = (jnp.dot(dquery_head, key_head.T, preferred_element_type=jnp.float32) + jnp.dot(query_head, dkey_head.T, preferred_element_type=jnp.float32)) * score_scale
    row_peak = lax.optimization_barrier(jnp.max(scores, axis=1, keepdims=True))
    weights = jnp.exp(scores - row_peak)
    row_total = lax.optimization_barrier(jnp.sum(weights, axis=1))
    mixed = weights * d_scores
    row_slope = lax.optimization_barrier(jnp.sum(mixed, axis=1))
    weights_low = weights.astype(jnp.bfloat16)
    mixed_low = mixed.astype(jnp.bfloat16)
    accum = jnp.dot(weights_low, value_head, preferred_element_type=jnp.float32)
    tangent = jnp.dot(mixed_low, value_head, preferred_element_type=jnp.float32) + jnp.dot(weights_low, dvalue_head, preferred_element_type=jnp.float32)
    attended = accum / row_total[:, None]
    d_attended = tangent / row_total[:, None] - (row_slope / row_total)[:, None] * attended
    return (attended, d_attended)

def split_heads(array):
    return array.reshape(LENGTH, HEADS, HEAD_DIM).transpose(1, 0, 2)

def reference(query, key, value, d_query, d_key, d_value, residual, d_residual, w_in, w_out):
    operands = tuple((split_heads(array) for array in (query, key, value, d_query, d_key, d_value)))
    attended, d_attended = lax.map(head_attend, operands)
    attended = attended.transpose(1, 0, 2).reshape(LENGTH, D)
    d_attended = d_attended.transpose(1, 0, 2).reshape(LENGTH, D)
    mixed_in = (residual.astype(jnp.float32) + attended).astype(jnp.bfloat16)
    d_mixed_in = (d_residual.astype(jnp.float32) + d_attended).astype(jnp.bfloat16)
    pre_act = jnp.dot(mixed_in, w_in, preferred_element_type=jnp.float32)
    d_pre_act = jnp.dot(d_mixed_in, w_in, preferred_element_type=jnp.float32)
    hidden, d_hidden = gelu_pair(pre_act, d_pre_act)
    hidden = hidden.astype(jnp.bfloat16)
    d_hidden = d_hidden.astype(jnp.bfloat16)
    block_out = (mixed_in.astype(jnp.float32) + jnp.dot(hidden, w_out, preferred_element_type=jnp.float32)).astype(jnp.bfloat16)
    d_block_out = (d_mixed_in.astype(jnp.float32) + jnp.dot(d_hidden, w_out, preferred_element_type=jnp.float32)).astype(jnp.bfloat16)
    return (block_out, d_block_out)
```

```python
import functools
import math

import jax
import jax.numpy as jnp
from jax import lax
from jax.experimental import pallas as pl
from jax.experimental.pallas import tpu as pltpu
from jax.sharding import PartitionSpec as P

HEAD_DIM = 128


gelu_coeff = 0.7978845608
cubic_coeff = 0.044715


def gelu_pair(pre_act, d_pre_act):
    inner_arg = gelu_coeff * (pre_act + cubic_coeff * pre_act * pre_act * pre_act)
    hyper = jnp.tanh(inner_arg)
    gelu_value = 0.5 * pre_act * (1.0 + hyper)
    gelu_slope = 0.5 * (1.0 + hyper) + 0.5 * pre_act * (1.0 - hyper * hyper) * gelu_coeff * (
        1.0 + 3.0 * cubic_coeff * pre_act * pre_act
    )
    return (gelu_value, gelu_slope * d_pre_act)


def nt(a, b):
    return lax.dot_general(a, b, (((1,), (1,)), ((), ())), preferred_element_type=jnp.float32)


def attend_math(q, dq, res, dres, keys, values, keys_pair, values_pair):
    scale = 1.0 / math.sqrt(HEAD_DIM)
    scores = nt(q, keys) * scale
    d_scores = nt(jnp.concatenate([dq, q], axis=1), keys_pair) * scale
    peak = jnp.max(scores, axis=1, keepdims=True)
    weights = jnp.exp(scores - peak)
    mixed = weights * d_scores
    total = jnp.sum(weights, axis=1, keepdims=True)
    slope = jnp.sum(mixed, axis=1, keepdims=True)
    both = jnp.dot(weights.astype(jnp.bfloat16), values_pair, preferred_element_type=jnp.float32)
    tangent = both[:, HEAD_DIM:] + jnp.dot(
        mixed.astype(jnp.bfloat16), values, preferred_element_type=jnp.float32
    )
    attended = both[:, :HEAD_DIM] / total
    d_attended = tangent / total - (slope / total) * attended
    return (
        (res.astype(jnp.float32) + attended).astype(jnp.bfloat16),
        (dres.astype(jnp.float32) + d_attended).astype(jnp.bfloat16),
    )


def attend_kernel(q, dq, res, dres, k, v, dk, dv, out, *, rows):
    keys, values = k[...], v[...]
    keys_pair = jnp.concatenate([keys, dk[...]], axis=1)
    values_pair = jnp.concatenate([values, dv[...]], axis=1)
    for start in range(0, q.shape[0], rows):
        part = pl.ds(start, rows)
        out[0, part, :], out[1, part, :] = attend_math(
            q[part, :], dq[part, :], res[part, :], dres[part, :],
            keys, values, keys_pair, values_pair,
        )


def attend(query, d_query, residual, d_residual, kv):
    rows, feats = query.shape
    heads = feats // HEAD_DIM
    length = kv.shape[0]
    own = pl.BlockSpec((rows, HEAD_DIM), lambda h: (0, h))

    def kv_spec(i):
        return pl.BlockSpec((length, HEAD_DIM), lambda h: (0, i * heads + h))

    return pl.pallas_call(
        functools.partial(attend_kernel, rows=min(rows, 128)),
        grid=(heads,),
        in_specs=[own] * 4 + [kv_spec(i) for i in range(4)],
        out_specs=pl.BlockSpec((2, rows, HEAD_DIM), lambda h: (0, 0, h)),
        out_shape=jax.ShapeDtypeStruct((2, rows, feats), jnp.bfloat16),
        cost_estimate=pl.CostEstimate(
            flops=12 * rows * length * feats, bytes_accessed=8 * length * feats, transcendentals=0
        ),
        name="attend",
    )(query, d_query, residual, d_residual, kv, kv, kv, kv)


def by_rows(query, key, value, d_query, d_key, d_value, residual, d_residual, w_in, w_out):
    rows, feats = query.shape
    kv = lax.all_gather(
        jnp.concatenate([key, value, d_key, d_value], axis=1), "seq", axis=0, tiled=True
    )
    w_in_whole = lax.all_gather(w_in, "seq", axis=0, tiled=True)
    w_out_whole = lax.all_gather(w_out, "seq", axis=0, tiled=True)
    mixed = attend(query, d_query, residual, d_residual, kv).reshape(2 * rows, feats)
    whole = lax.all_gather(mixed, "dp", axis=1, tiled=True)
    pre = jnp.dot(whole, w_in_whole, preferred_element_type=jnp.float32)
    hidden, d_hidden = gelu_pair(pre[:rows], pre[rows:])
    hidden = jnp.concatenate([hidden.astype(jnp.bfloat16), d_hidden.astype(jnp.bfloat16)], axis=0)
    partial = jnp.dot(hidden, w_out_whole, preferred_element_type=jnp.float32)
    summed = lax.psum_scatter(
        partial.astype(jnp.bfloat16), "dp", scatter_dimension=1, tiled=True
    ).astype(jnp.float32)
    out = (mixed.astype(jnp.float32) + summed).astype(jnp.bfloat16)
    return (out[:rows], out[rows:])


INNER = 4
MESH = pl.DeviceIdType.MESH
COMM_COST = pl.CostEstimate(flops=10**11, bytes_accessed=10**8, transcendentals=0)


def place(groups):
    seq = lax.axis_index("seq")
    return lax.axis_index("dp"), lax.div(seq, INNER), lax.rem(seq, INNER)


def enter(devices):
    barrier = pltpu.get_barrier_semaphore()
    for device in devices:
        pl.semaphore_signal(barrier, inc=1, device_id=device, device_id_type=MESH)
    pl.semaphore_wait(barrier, len(devices))


def block_kernel(
    q, dq, res, dres, k, v, dk, dv, w_in, w_out, out_main, out_tangent,
    own, kv, wl, wol, mix, gat, left, hid, part, arrived, fin,
    z_send, z_recv, own_sem, ky_send, ky_recv, kp_send, kp_recv, kf_send, kf_recv,
    wz_send, wz_recv, gi_send, gi_recv, go_send, go_recv, w_sem,
    swap_send, swap_recv, mine_sem, right_send, right_recv, left_send, left_recv,
    rs_send, rs_recv, out_send, out_recv, out_sem,
):
    groups, width = own.shape[1], own.shape[3]
    feats = q.shape[1]
    hidden = w_in.shape[1] // groups
    heads = width // HEAD_DIM
    half = mix.shape[4]
    last = groups - 1
    slices = fin.shape[0]
    span = fin.shape[3]
    parts = go_send.shape[0]
    deep_out = w_out.shape[0] // parts
    homes = ((1, 2), (0, 3))
    x, g, i = place(groups)
    other = 1 - x
    core = lax.rem(i, 2)
    next_i = i + 1 - 2 * core
    across_i = lax.rem(i + 2, INNER)
    partner = (x, g * INNER + next_i)
    across = (x, g * INNER + across_i)
    twin = (other, g * INNER + i)
    peers = [(x, lax.rem(g + t, groups) * INNER + i) for t in range(1, groups)]
    up = (x, jnp.minimum(g + 1, last) * INNER + i)
    down = (x, jnp.maximum(g - 1, 0) * INNER + i)
    enter(peers + [partner, across, twin])

    def remote(src, dst, send, recv, device):
        return pltpu.make_async_remote_copy(
            src_ref=src, dst_ref=dst, send_sem=send, recv_sem=recv,
            device_id=device, device_id_type=MESH,
        )

    sent = []

    def go(copy):
        copy.start()
        sent.append(copy)
        return copy

    def source_of(t):
        return lax.rem(g + groups - t, groups)

    def piece(j, to):
        ref = (k, v, dk, dv, q, dq, res, dres)[j]
        return ref.at[:, pl.ds(pl.multiple_of(to * width, 128), width)]

    def slot(j, source):
        return kv.at[i, source, j] if j < 4 else own.at[j - 4, source]

    z_copies = {}

    def z_start(t, j):
        z_copies[t, j] = go(remote(
            piece(j, lax.rem(g + t, groups)), slot(j, g),
            z_send.at[t - 1, j], z_recv.at[t - 1, j], peers[t - 1],
        ))

    def w_in_piece(to):
        return w_in.at[:, pl.ds(pl.multiple_of(to * hidden, 128), hidden)]

    def w_in_slot(xs, at, s):
        return wl.at[s, at, :, pl.ds(pl.multiple_of(xs * hidden, 128), hidden)]

    def w_out_slot(xs, at, r):
        return wol.at[xs, at, pl.ds(r * deep_out, deep_out)]

    def gather(slot_of, send, recv, first, second, first_at, second_at):
        def copy(which, src_at, n, idx, device, src=None):
            dst = slot_of(src_at[0], src_at[1], n)
            return remote(src if src is not None else dst, dst,
                          send.at[idx, which], recv.at[idx, which], device)

        def start(n, idx, src=None):
            me = (x, i)
            go(copy(0, me, n, idx, first, src))
            go(copy(1, me, n, idx, second, src))
            go(copy(2, me, n, idx, partner, src))

        def wait(which, at, n, idx):
            copy(which, at, n, idx, partner).wait_recv()

        def from_first(n, idx):
            wait(0, first_at, n, idx)
            go(copy(3, first_at, n, idx, second))
            go(copy(4, first_at, n, idx, partner))

        def from_second(n, idx):
            wait(1, second_at, n, idx)
            go(copy(5, second_at, n, idx, partner))

        def from_far(n, idx):
            far = (other, across_i)
            wait(3, far, n, idx)
            go(copy(6, far, n, idx, partner))

        def finish(n, idx):
            for which, at in ((2, (x, i)), (4, first_at), (5, second_at), (6, (other, across_i))):
                wait(which, (at[0], at[1] + 1 - 2 * lax.rem(at[1], 2)), n, idx)

        return start, from_first, from_second, from_far, finish

    def pick(a, b):
        return tuple(jnp.where(core == 0, m, n) for m, n in zip(a, b))

    go_start, go_first, go_second, go_far, go_finish = gather(
        w_out_slot, go_send, go_recv, pick(twin, across), pick(across, twin),
        pick((other, i), (x, across_i)), pick((x, across_i), (other, i)),
    )
    gi_start, gi_first, gi_second, gi_far, gi_finish = gather(
        w_in_slot, gi_send, gi_recv, across, twin, (x, across_i), (other, i),
    )

    wz = {}

    def wz_start(t):
        wz[t] = go(remote(
            w_in_piece(lax.rem(g + t, groups)), w_in_slot(x, i, g),
            wz_send.at[t - 1], wz_recv.at[t - 1], peers[t - 1],
        ))

    def kv_copy(at, source, send, recv, t, device):
        return remote(kv.at[at, source], kv.at[at, source], send.at[t], recv.at[t], device)

    def kv_spread(t):
        go(kv_copy(i, source_of(t), ky_send, ky_recv, t, across))
        go(kv_copy(i, source_of(t), kp_send, kp_recv, t, partner))

    def kv_forward(t):
        kv_copy(across_i, source_of(t), ky_send, ky_recv, t, across).wait_recv()
        go(kv_copy(across_i, source_of(t), kf_send, kf_recv, t, partner))

    def kv_finish(t):
        kv_copy(next_i, source_of(t), kp_send, kp_recv, t, partner).wait_recv()
        at = across_i + 1 - 2 * lax.rem(across_i, 2)
        kv_copy(at, source_of(t), kf_send, kf_recv, t, partner).wait_recv()

    def attend_head(chunk, h):
        feat = pl.ds(h * HEAD_DIM, HEAD_DIM)
        length = kv.shape[0] * kv.shape[1] * kv.shape[3]
        keys, values, d_keys, d_values = (
            kv[:, :, j, :, feat].reshape(length, HEAD_DIM) for j in range(4)
        )
        keys_pair = jnp.concatenate([keys, d_keys], axis=1)
        values_pair = jnp.concatenate([values, d_values], axis=1)
        for c in range(2):
            home = homes[chunk][c]
            pair = attend_math(
                own[0, home, :, feat], own[1, home, :, feat],
                own[2, home, :, feat], own[3, home, :, feat],
                keys, values, keys_pair, values_pair,
            )
            for side in range(2):
                for kind in range(2):
                    mix[side, chunk, kind, c, :, feat] = pair[kind][side * half : (side + 1) * half]

    def swap(chunk):
        return remote(mix.at[other, chunk], gat.at[chunk, g, x],
                      swap_send.at[chunk], swap_recv.at[chunk], twin)

    def hop(chunk, c, t, to_right):
        source = g - t if to_right else g + t
        sends, recvs = (right_send, right_recv) if to_right else (left_send, left_recv)
        side = other if c else x
        return remote(
            mix.at[x, chunk] if c == 0 and t == 0 else gat.at[chunk, source, side],
            gat.at[chunk, source, side],
            sends.at[chunk, c, t], recvs.at[chunk, c, t], up if to_right else down,
        )

    def sends_right(t):
        return (g >= t) & (g < last)

    def sends_left(t):
        return (g + t <= last) & (g > 0)

    def line_step(chunk, c, t):
        if t == 0 and c:
            swap(chunk).wait_recv()
        if t:

            @pl.when(g >= t)
            def _():
                hop(chunk, c, t - 1, True).wait_recv()

            @pl.when(g + t <= last)
            def _():
                hop(chunk, c, t - 1, False).wait_recv()

        if t < last:

            @pl.when(sends_right(t))
            def _():
                hop(chunk, c, t, True).start()

            @pl.when(sends_left(t))
            def _():
                hop(chunk, c, t, False).start()

    mine = {}

    def line_start(chunk):
        go(swap(chunk))
        mine[chunk] = pltpu.make_async_copy(mix.at[x, chunk], gat.at[chunk, g, x], mine_sem.at[chunk])
        mine[chunk].start()
        line_step(chunk, 0, 0)

    def line_sent(chunk):
        for c in range(2):
            for t in range(last):

                @pl.when(sends_right(t))
                def _():
                    hop(chunk, c, t, True).wait_send()

                @pl.when(sends_left(t))
                def _():
                    hop(chunk, c, t, False).wait_send()

    def hidden_chunk(chunk):
        rows = hid.shape[0]
        for xs in range(2):
            for s in range(groups):
                start = (xs * groups + s) * width
                left[:, start : start + width] = gat[chunk, s, xs].reshape(rows, width)
        tile = 256
        deep = left.shape[1]

        def body(n, carry):
            columns = pl.ds(pl.multiple_of(n * tile, tile), tile)
            total = jnp.dot(
                left[...], wl[:, :, :, columns].reshape(deep, tile), preferred_element_type=jnp.float32
            )
            value, tangent = gelu_pair(total[: rows // 2], total[rows // 2 :])
            hid[: rows // 2, columns] = value.astype(jnp.bfloat16)
            hid[rows // 2 :, columns] = tangent.astype(jnp.bfloat16)
            return carry

        lax.fori_loop(0, hid.shape[1] // tile, body, 0)

    def out_slice(chunk, n):
        deep = hid.shape[1]
        tile = 256
        for m in range(span // tile):
            start = n * span + m * tile
            total = jnp.dot(
                hid[...], wol[:, :, :, start : start + tile].reshape(deep, tile),
                preferred_element_type=jnp.float32,
            ).astype(jnp.bfloat16)
            for kind in range(2):
                for c in range(2):
                    at = (kind * 2 + c) * half
                    part[chunk, c, n, kind, :, m * tile : (m + 1) * tile] = total[at : at + half]

    def sum_copy(to_up, chunk, c, n):
        way = 0 if to_up else 1
        return remote(
            part.at[chunk, c, n], arrived.at[way, chunk, c, n],
            rs_send.at[way, chunk, c, n], rs_recv.at[way, chunk, c, n], up if to_up else down,
        )

    def add_in(to_up, chunk, c, n):
        sum_copy(to_up, chunk, c, n).wait_recv()
        way = 0 if to_up else 1
        part[chunk, c, n] = (
            part[chunk, c, n].astype(jnp.float32) + arrived[way, chunk, c, n].astype(jnp.float32)
        ).astype(jnp.bfloat16)

    def sum_start(chunk, n):
        for c in range(2):
            home = homes[chunk][c]
            if home > 0:

                @pl.when(g == 0)
                def _():
                    sum_copy(True, chunk, c, n).start()

            if home < last:

                @pl.when(g == last)
                def _():
                    sum_copy(False, chunk, c, n).start()

    def sum_step(chunk, n, distance):
        for c in range(2):
            home = homes[chunk][c]
            if distance < home:

                @pl.when(g == distance)
                def _():
                    add_in(True, chunk, c, n)
                    sum_copy(True, chunk, c, n).start()

            if last - distance > home:

                @pl.when(g == last - distance)
                def _():
                    add_in(False, chunk, c, n)
                    sum_copy(False, chunk, c, n).start()

    def out_copies(n, local):
        side, start = divmod(n * span, feats)
        made = []
        for kind, ref in enumerate((out_main, out_tangent)):
            dst = ref.at[pl.ds(pl.multiple_of(x * half, half), half), pl.ds(start, span)]
            if local:
                made.append(pltpu.make_async_copy(fin.at[n, kind], dst, out_sem.at[n, kind]))
            else:
                made.append(remote(fin.at[n, kind], dst, out_send.at[n, kind], out_recv.at[n, kind], twin))
        return side, made

    def sum_final(chunk, n):
        for c in range(2):
            home = homes[chunk][c]

            @pl.when(g == home)
            def _():
                total = part[chunk, c, n].astype(jnp.float32)
                for way, needed in ((0, home > 0), (1, home < last)):
                    if needed:
                        sum_copy(way == 0, chunk, c, n).wait_recv()
                        total = total + arrived[way, chunk, c, n].astype(jnp.float32)
                for kind in range(2):
                    at = (kind * 2 + c) * half
                    for m in range(span // width):
                        s = (n * span % feats) // width + m
                        fin[n, kind, :, m * width : (m + 1) * width] = (
                            gat[chunk, s, n * span // feats, kind, c].astype(jnp.float32)
                            + total[kind, :, m * width : (m + 1) * width]
                        ).astype(jnp.bfloat16)
                side, local = out_copies(n, True)
                _, far = out_copies(n, False)

                @pl.when(x == side)
                def _():
                    for copy in local:
                        copy.start()

                @pl.when(x != side)
                def _():
                    for copy in far:
                        copy.start()

    for t in range(1, groups):
        for j in range(8):
            z_start(t, j)
    locals_ = [pltpu.make_async_copy(piece(j, g), slot(j, g), own_sem.at[j]) for j in range(8)]
    for copy in locals_:
        copy.start()
    w_locals = [
        pltpu.make_async_copy(w_in_piece(g), w_in_slot(x, i, g), w_sem.at[0]),
        pltpu.make_async_copy(w_out, wol.at[x, i], w_sem.at[1]),
    ]
    for copy in w_locals:
        copy.start()
    for copy in locals_:
        copy.wait()
    kv_spread(0)
    for r in range(parts):
        go_start(r, r, w_out.at[pl.ds(r * deep_out, deep_out)])
    for t in range(1, groups):
        wz_start(t)
    kv_forward(0)
    gi_start(g, 0, w_in_piece(g))
    for t in range(1, groups):
        for j in range(4):
            z_copies[t, j].wait_recv()
        kv_spread(t)
        if t - 1 < parts:
            go_first(t - 1, t - 1)
        if t > 1:
            kv_forward(t - 1)
    for r in range(groups - 1, parts):
        go_first(r, r)
    kv_forward(groups - 1)
    for t in range(groups):
        kv_finish(t)
    for t in range(1, groups):
        for j in range(4, 8):
            z_copies[t, j].wait_recv()
    gi_first(g, 0)
    for h in range(heads):
        attend_head(0, h)
    line_start(0)
    for r in range(parts):
        go_second(r, r)
        go_far(r, r)
    gi_second(g, 0)
    gi_far(g, 0)
    for h in range(heads):
        attend_head(1, h)
    line_step(0, 1, 0)
    line_start(1)
    for t in range(1, groups):
        wz[t].wait_recv()
        gi_start(source_of(t), t)
        line_step(0, 0, t)
        line_step(0, 1, t)
    line_step(1, 1, 0)
    for t in range(1, groups):
        gi_first(source_of(t), t)
    for t in range(1, groups):
        gi_second(source_of(t), t)
        gi_far(source_of(t), t)
    line_step(1, 0, 1)
    for copy in w_locals:
        copy.wait()
    for t in range(groups):
        gi_finish(source_of(t), t)
    mine[0].wait()
    hidden_chunk(0)
    line_step(1, 1, 1)
    for r in range(parts):
        go_finish(r, r)
    order = [n for pair in zip(range(slices // 2), range(slices // 2, slices)) for n in pair]
    for n in order:
        out_slice(0, n)
        sum_start(0, n)
    line_step(1, 0, 2)
    line_step(1, 1, 2)
    line_step(1, 0, 3)
    line_step(1, 1, 3)
    mine[1].wait()
    hidden_chunk(1)
    for n in order:
        sum_step(0, n, 1)
    for n in order:
        out_slice(1, n)
        sum_start(1, n)
    for n in order:
        sum_final(0, n)
    for n in order:
        sum_step(1, n, 1)
    for n in order:
        sum_step(1, n, 2)
    for n in order:
        sum_final(1, n)
    for n in range(slices):
        side, local = out_copies(n, True)
        _, far = out_copies(n, False)

        @pl.when(x == side)
        def _():
            for copy in local:
                copy.wait()
            for copy in far:
                copy.wait_recv()

        @pl.when(x != side)
        def _():
            for copy in far:
                copy.wait_send()

    for copy in sent:
        copy.wait_send()
    for chunk in range(2):
        line_sent(chunk)
        for c in range(2):
            home = homes[chunk][c]
            for n in range(slices):

                @pl.when(g < home)
                def _():
                    sum_copy(True, chunk, c, n).wait_send()

                @pl.when(g > home)
                def _():
                    sum_copy(False, chunk, c, n).wait_send()


SLICES = 4
PARTS = 2


def by_layers(query, key, value, d_query, d_key, d_value, residual, d_residual, w_in, w_out, dp, seq):
    groups = seq // INNER
    rows, feats = query.shape
    half, width = rows // dp, feats // groups
    deep, hidden = w_in.shape[0], w_in.shape[1] // groups
    whole = dp * feats
    span = whole // SLICES
    dma = pltpu.SemaphoreType.DMA
    low = jnp.bfloat16
    last = groups - 1
    length = groups * INNER * rows
    flops = 12 * groups * rows * length * width + 8 * dp * hidden * whole * groups * half * 2
    return tuple(pl.pallas_call(
        block_kernel,
        in_specs=[pl.BlockSpec(memory_space=pl.ANY)] * 10,
        out_specs=[pl.BlockSpec(memory_space=pl.ANY)] * 2,
        out_shape=[jax.ShapeDtypeStruct((rows, feats), low)] * 2,
        scratch_shapes=[
            pltpu.VMEM((4, groups, rows, width), low),
            pltpu.VMEM((INNER, groups, 4, rows, width), low),
            pltpu.VMEM((groups, INNER, deep, dp * hidden), low),
            pltpu.VMEM((dp, INNER, w_out.shape[0], whole), low),
            pltpu.VMEM((dp, 2, 2, 2, half, width), low),
            pltpu.VMEM((2, groups, dp, 2, 2, half, width), low),
            pltpu.VMEM((4 * half, whole), low),
            pltpu.VMEM((4 * half, dp * hidden), low),
            pltpu.VMEM((2, 2, SLICES, 2, half, span), low),
            pltpu.VMEM((2, 2, 2, SLICES, 2, half, span), low),
            pltpu.VMEM((SLICES, 2, half, span), low),
            dma((last, 8)), dma((last, 8)), dma((8,)),
        ]
        + [dma((groups,)) for _ in range(6)]
        + [dma((last,)), dma((last,)), dma((groups, 7)), dma((groups, 7)), dma((PARTS, 7)), dma((PARTS, 7)), dma((2,))]
        + [dma((2,)), dma((2,)), dma((2,))]
        + [dma((2, 2, last)) for _ in range(4)]
        + [dma((2, 2, 2, SLICES)), dma((2, 2, 2, SLICES))]
        + [dma((SLICES, 2)) for _ in range(3)],
        cost_estimate=pl.CostEstimate(flops=flops, bytes_accessed=10**8, transcendentals=0),
        compiler_params=pltpu.CompilerParams(
            collective_id=0, has_side_effects=True, vmem_limit_bytes=60 * 2**20
        ),
        name="block",
    )(query, d_query, residual, d_residual, key, value, d_key, d_value, w_in, w_out))


def on_device(*args, dp, seq):
    query, w_in = args[0], args[8]
    groups = seq // INNER
    tile = groups * HEAD_DIM
    if dp != 2 or seq % INNER or groups != 4 or query.shape[1] % tile or w_in.shape[1] % tile:
        return by_rows(*args)
    return by_layers(*args, dp=dp, seq=seq)


def solution(mesh):
    in_specs = (P("seq", "dp"),) * 9 + (P(("dp", "seq"), None),)
    out_specs = (P("seq", "dp"), P("seq", "dp"))
    body = functools.partial(on_device, dp=mesh.shape["dp"], seq=mesh.shape["seq"])
    return jax.shard_map(
        body, mesh=mesh, in_specs=in_specs, out_specs=out_specs, check_vma=False
    )
```

```python
import functools
import math

import jax
import jax.numpy as jnp
from jax import lax
from jax.experimental import pallas as pl
from jax.experimental.pallas import tpu as pltpu
from jax.sharding import PartitionSpec as P

HEAD_DIM = 128


gelu_coeff = 0.7978845608
cubic_coeff = 0.044715


def gelu_pair(pre_act, d_pre_act):
    inner_arg = gelu_coeff * (pre_act + cubic_coeff * pre_act * pre_act * pre_act)
    hyper = jnp.tanh(inner_arg)
    gelu_value = 0.5 * pre_act * (1.0 + hyper)
    gelu_slope = 0.5 * (1.0 + hyper) + 0.5 * pre_act * (1.0 - hyper * hyper) * gelu_coeff * (
        1.0 + 3.0 * cubic_coeff * pre_act * pre_act
    )
    return (gelu_value, gelu_slope * d_pre_act)


def nt(a, b):
    return lax.dot_general(a, b, (((1,), (1,)), ((), ())), preferred_element_type=jnp.float32)


def attend_math(q, dq, res, dres, keys, values, keys_pair, values_pair):
    scale = 1.0 / math.sqrt(HEAD_DIM)
    scores = nt(q, keys) * scale
    d_scores = nt(jnp.concatenate([dq, q], axis=1), keys_pair) * scale
    peak = jnp.max(scores, axis=1, keepdims=True)
    weights = jnp.exp(scores - peak)
    mixed = weights * d_scores
    total = jnp.sum(weights, axis=1, keepdims=True)
    slope = jnp.sum(mixed, axis=1, keepdims=True)
    both = jnp.dot(weights.astype(jnp.bfloat16), values_pair, preferred_element_type=jnp.float32)
    tangent = both[:, HEAD_DIM:] + jnp.dot(
        mixed.astype(jnp.bfloat16), values, preferred_element_type=jnp.float32
    )
    attended = both[:, :HEAD_DIM] / total
    d_attended = tangent / total - (slope / total) * attended
    return (
        (res.astype(jnp.float32) + attended).astype(jnp.bfloat16),
        (dres.astype(jnp.float32) + d_attended).astype(jnp.bfloat16),
    )


def attend_kernel(q, dq, res, dres, k, v, dk, dv, out, *, rows):
    keys, values = k[...], v[...]
    keys_pair = jnp.concatenate([keys, dk[...]], axis=1)
    values_pair = jnp.concatenate([values, dv[...]], axis=1)
    for start in range(0, q.shape[0], rows):
        part = pl.ds(start, rows)
        out[0, part, :], out[1, part, :] = attend_math(
            q[part, :], dq[part, :], res[part, :], dres[part, :],
            keys, values, keys_pair, values_pair,
        )


def attend(query, d_query, residual, d_residual, kv):
    rows, feats = query.shape
    heads = feats // HEAD_DIM
    length = kv.shape[0]
    own = pl.BlockSpec((rows, HEAD_DIM), lambda h: (0, h))

    def kv_spec(i):
        return pl.BlockSpec((length, HEAD_DIM), lambda h: (0, i * heads + h))

    return pl.pallas_call(
        functools.partial(attend_kernel, rows=min(rows, 128)),
        grid=(heads,),
        in_specs=[own] * 4 + [kv_spec(i) for i in range(4)],
        out_specs=pl.BlockSpec((2, rows, HEAD_DIM), lambda h: (0, 0, h)),
        out_shape=jax.ShapeDtypeStruct((2, rows, feats), jnp.bfloat16),
        cost_estimate=pl.CostEstimate(
            flops=12 * rows * length * feats, bytes_accessed=8 * length * feats, transcendentals=0
        ),
        name="attend",
    )(query, d_query, residual, d_residual, kv, kv, kv, kv)


def by_rows(query, key, value, d_query, d_key, d_value, residual, d_residual, w_in, w_out):
    rows, feats = query.shape
    kv = lax.all_gather(
        jnp.concatenate([key, value, d_key, d_value], axis=1), "seq", axis=0, tiled=True
    )
    w_in_whole = lax.all_gather(w_in, "seq", axis=0, tiled=True)
    w_out_whole = lax.all_gather(w_out, "seq", axis=0, tiled=True)
    mixed = attend(query, d_query, residual, d_residual, kv).reshape(2 * rows, feats)
    whole = lax.all_gather(mixed, "dp", axis=1, tiled=True)
    pre = jnp.dot(whole, w_in_whole, preferred_element_type=jnp.float32)
    hidden, d_hidden = gelu_pair(pre[:rows], pre[rows:])
    hidden = jnp.concatenate([hidden.astype(jnp.bfloat16), d_hidden.astype(jnp.bfloat16)], axis=0)
    partial = jnp.dot(hidden, w_out_whole, preferred_element_type=jnp.float32)
    summed = lax.psum_scatter(
        partial.astype(jnp.bfloat16), "dp", scatter_dimension=1, tiled=True
    ).astype(jnp.float32)
    out = (mixed.astype(jnp.float32) + summed).astype(jnp.bfloat16)
    return (out[:rows], out[rows:])


INNER = 4
MESH = pl.DeviceIdType.MESH
COMM_COST = pl.CostEstimate(flops=10**11, bytes_accessed=10**8, transcendentals=0)


def place(groups):
    seq = lax.axis_index("seq")
    return lax.axis_index("dp"), lax.div(seq, INNER), lax.rem(seq, INNER)


def enter(devices):
    barrier = pltpu.get_barrier_semaphore()
    for device in devices:
        pl.semaphore_signal(barrier, inc=1, device_id=device, device_id_type=MESH)
    pl.semaphore_wait(barrier, len(devices))


def block_kernel(
    q, dq, res, dres, k, v, dk, dv, w_in, w_out, out_main, out_tangent,
    own, kv, wl, wol, mix, gat, left, hid, part, arrived, fin,
    z_send, z_recv, own_sem, ky_send, ky_recv, kp_send, kp_recv, kf_send, kf_recv,
    wz_send, wz_recv, gi_send, gi_recv, go_send, go_recv, w_sem,
    swap_send, swap_recv, mine_sem, right_send, right_recv, left_send, left_recv,
    rs_send, rs_recv, out_send, out_recv, out_sem,
):
    groups, width = own.shape[1], own.shape[3]
    feats = q.shape[1]
    hidden = w_in.shape[1] // groups
    heads = width // HEAD_DIM
    half = mix.shape[4]
    last = groups - 1
    slices = fin.shape[0]
    span = fin.shape[3]
    parts = go_send.shape[0]
    wide_out = w_out.shape[1] // parts
    cuts = wz_send.shape[1]
    deep_in = w_in.shape[0] // cuts
    homes = ((1, 2), (0, 3))
    x, g, i = place(groups)
    other = 1 - x
    core = lax.rem(i, 2)
    next_i = i + 1 - 2 * core
    across_i = lax.rem(i + 2, INNER)
    partner = (x, g * INNER + next_i)
    across = (x, g * INNER + across_i)
    twin = (other, g * INNER + i)
    high = lax.div(g, 2)
    ranks = (last * (1 - high), 2 - high, g + 1 - 2 * lax.rem(g, 2), g)
    peers = [(x, to * INNER + i) for to in ranks[:last]]
    up = (x, jnp.minimum(g + 1, last) * INNER + i)
    down = (x, jnp.maximum(g - 1, 0) * INNER + i)
    enter(peers + [partner, across, twin])

    def remote(src, dst, send, recv, device):
        return pltpu.make_async_remote_copy(
            src_ref=src, dst_ref=dst, send_sem=send, recv_sem=recv,
            device_id=device, device_id_type=MESH,
        )

    sent = []

    def go(copy):
        copy.start()
        sent.append(copy)
        return copy

    def piece(j, to):
        ref = (k, v, dk, dv, q, dq, res, dres)[j]
        return ref.at[:, pl.ds(pl.multiple_of(to * width, 128), width)]

    def slot(j, source):
        return kv.at[i, source, j] if j < 4 else own.at[j - 4, source]

    def z_start(r, j):
        go(remote(piece(j, ranks[r]), slot(j, g), z_send.at[r, j], z_recv.at[g, j], peers[r]))

    def z_wait(r, j):
        source = ranks[r]
        remote(piece(j, source), slot(j, source), z_send.at[r, j], z_recv.at[source, j], peers[r]).wait_recv()

    def w_in_piece(to, p):
        return w_in.at[pl.ds(p * deep_in, deep_in), pl.ds(pl.multiple_of(to * hidden, 128), hidden)]

    def w_in_slot(xs, at, n):
        s, p = n
        columns = pl.ds(pl.multiple_of(xs * hidden, 128), hidden)
        return wl.at[s, at, pl.ds(p * deep_in, deep_in), columns]

    def w_out_piece(r):
        return w_out.at[:, pl.ds(r * wide_out, wide_out)]

    def w_out_slot(xs, at, r):
        return wol.at[xs, at, :, pl.ds(r * wide_out, wide_out)]

    def gather(slot_of, send, recv, first, second, first_at, second_at):
        def copy(which, src_at, n, idx, device, src=None):
            dst = slot_of(src_at[0], src_at[1], n)
            at = idx if isinstance(idx, tuple) else (idx,)
            return remote(src if src is not None else dst, dst,
                          send.at[at + (which,)], recv.at[at + (which,)], device)

        def start(n, idx, src=None):
            me = (x, i)
            go(copy(0, me, n, idx, first, src))
            go(copy(1, me, n, idx, second, src))
            go(copy(2, me, n, idx, partner, src))

        def wait(which, at, n, idx):
            copy(which, at, n, idx, partner).wait_recv()

        def from_first(n, idx):
            wait(0, first_at, n, idx)
            go(copy(3, first_at, n, idx, second))
            go(copy(4, first_at, n, idx, partner))

        def from_second(n, idx):
            wait(1, second_at, n, idx)
            go(copy(5, second_at, n, idx, partner))

        def from_far(n, idx):
            far = (other, across_i)
            wait(3, far, n, idx)
            go(copy(6, far, n, idx, partner))

        def finish(n, idx):
            for which, at in ((2, (x, i)), (4, first_at), (5, second_at), (6, (other, across_i))):
                wait(which, (at[0], at[1] + 1 - 2 * lax.rem(at[1], 2)), n, idx)

        return start, from_first, from_second, from_far, finish

    def pick(a, b):
        return tuple(jnp.where(core == 0, m, n) for m, n in zip(a, b))

    go_start, go_first, go_second, go_far, go_finish = gather(
        w_out_slot, go_send, go_recv, across, twin, (x, across_i), (other, i),
    )
    gi_start, gi_first, gi_second, gi_far, gi_finish = gather(
        w_in_slot, gi_send, gi_recv, pick(twin, across), pick(across, twin),
        pick((other, i), (x, across_i)), pick((x, across_i), (other, i)),
    )

    def wz_start(r, p):
        return remote(
            w_in_piece(ranks[r], p), w_in_slot(x, i, (g, p)),
            wz_send.at[r, p], wz_recv.at[g, p], peers[r],
        )

    def w_in_first(t, p):
        gi_first((ranks[t], p), (t, p))

    def w_in_rest(t, p):
        gi_second((ranks[t], p), (t, p))
        gi_far((ranks[t], p), (t, p))

    def w_in_start(t, p):
        source = ranks[t]
        remote(
            w_in_piece(source, p), w_in_slot(x, i, (source, p)),
            wz_send.at[t, p], wz_recv.at[source, p], peers[t],
        ).wait_recv()
        gi_start((ranks[t], p), (t, p))

    def w_out_rest(r):
        go_second(r, r)
        go_far(r, r)

    def kv_copy(at, t, j, send, recv, device):
        block = kv.at[at, ranks[t], j]
        return remote(block, block, send.at[t, j], recv.at[t, j], device)

    def kv_spread(t, j):
        go(kv_copy(i, t, j, ky_send, ky_recv, across))
        go(kv_copy(i, t, j, kp_send, kp_recv, partner))

    def kv_forward(t, j):
        kv_copy(across_i, t, j, ky_send, ky_recv, across).wait_recv()
        go(kv_copy(across_i, t, j, kf_send, kf_recv, partner))

    def kv_finish(t, j):
        kv_copy(next_i, t, j, kp_send, kp_recv, partner).wait_recv()
        at = across_i + 1 - 2 * lax.rem(across_i, 2)
        kv_copy(at, t, j, kf_send, kf_recv, partner).wait_recv()

    def attend_head(chunk, h):
        feat = pl.ds(h * HEAD_DIM, HEAD_DIM)
        length = kv.shape[0] * kv.shape[1] * kv.shape[3]
        keys, values, d_keys, d_values = (
            kv[:, :, j, :, feat].reshape(length, HEAD_DIM) for j in range(4)
        )
        keys_pair = jnp.concatenate([keys, d_keys], axis=1)
        values_pair = jnp.concatenate([values, d_values], axis=1)
        for c in range(2):
            home = homes[chunk][c]
            pair = attend_math(
                own[0, home, :, feat], own[1, home, :, feat],
                own[2, home, :, feat], own[3, home, :, feat],
                keys, values, keys_pair, values_pair,
            )
            for side in range(2):
                for kind in range(2):
                    mix[side, chunk, kind, c, :, feat] = pair[kind][side * half : (side + 1) * half]

    def swap(chunk):
        return remote(mix.at[other, chunk], gat.at[chunk, g, x],
                      swap_send.at[chunk], swap_recv.at[chunk], twin)

    def hop(chunk, c, t, to_right):
        source = g - t if to_right else g + t
        sends, recvs = (right_send, right_recv) if to_right else (left_send, left_recv)
        side = other if c else x
        return remote(
            mix.at[x, chunk] if c == 0 and t == 0 else gat.at[chunk, source, side],
            gat.at[chunk, source, side],
            sends.at[chunk, c, t], recvs.at[chunk, c, t], up if to_right else down,
        )

    def sends_right(t):
        return (g >= t) & (g < last)

    def sends_left(t):
        return (g + t <= last) & (g > 0)

    def line_step(chunk, c, t):
        if t == 0 and c:
            swap(chunk).wait_recv()
        if t:

            @pl.when(g >= t)
            def _():
                hop(chunk, c, t - 1, True).wait_recv()

            @pl.when(g + t <= last)
            def _():
                hop(chunk, c, t - 1, False).wait_recv()

        if t < last:

            @pl.when(sends_right(t))
            def _():
                hop(chunk, c, t, True).start()

            @pl.when(sends_left(t))
            def _():
                hop(chunk, c, t, False).start()

    mine = {}

    def swap_start(chunk):
        go(swap(chunk))
        mine[chunk] = pltpu.make_async_copy(mix.at[x, chunk], gat.at[chunk, g, x], mine_sem.at[chunk])
        mine[chunk].start()

    def line_sent(chunk):
        for c in range(2):
            for t in range(last):

                @pl.when(sends_right(t))
                def _():
                    hop(chunk, c, t, True).wait_send()

                @pl.when(sends_left(t))
                def _():
                    hop(chunk, c, t, False).wait_send()

    def hidden_left(chunk):
        for xs in range(2):
            for s in range(groups):
                start = (xs * groups + s) * width
                left[:, start : start + width] = gat[chunk, s, xs].reshape(hid.shape[0], width)

    def hidden_tile(n):
        rows, tile = hid.shape[0], HIDDEN_TILE
        columns = slice(n * tile, (n + 1) * tile)
        total = jnp.dot(
            left[...], wl[:, :, :, columns].reshape(left.shape[1], tile),
            preferred_element_type=jnp.float32,
        )
        value, tangent = gelu_pair(total[: rows // 2], total[rows // 2 :])
        hid[: rows // 2, columns] = value.astype(jnp.bfloat16)
        hid[rows // 2 :, columns] = tangent.astype(jnp.bfloat16)

    def out_slices(chunk, m):
        wide = 2 * span
        total = jnp.dot(
            hid[...], wol[:, :, :, m * wide : (m + 1) * wide].reshape(hid.shape[1], wide),
            preferred_element_type=jnp.float32,
        ).astype(jnp.bfloat16)
        for kind in range(2):
            for c in range(2):
                at = (kind * 2 + c) * half
                for n in range(2):
                    part[chunk, c, 2 * m + n, kind] = total[at : at + half, n * span : (n + 1) * span]

    def sum_copy(to_up, chunk, c, n):
        way = 0 if to_up else 1
        return remote(
            part.at[chunk, c, n], arrived.at[way, chunk, c, n],
            rs_send.at[way, chunk, c, n], rs_recv.at[way, chunk, c, n], up if to_up else down,
        )

    def add_in(to_up, chunk, c, n):
        sum_copy(to_up, chunk, c, n).wait_recv()
        way = 0 if to_up else 1
        part[chunk, c, n] = (
            part[chunk, c, n].astype(jnp.float32) + arrived[way, chunk, c, n].astype(jnp.float32)
        ).astype(jnp.bfloat16)

    def sum_start(chunk, n, distance):
        for c in range(2):
            home = homes[chunk][c]
            if home == distance:

                @pl.when(g == 0)
                def _():
                    sum_copy(True, chunk, c, n).start()

            if home == last - distance:

                @pl.when(g == last)
                def _():
                    sum_copy(False, chunk, c, n).start()

    def sum_step(chunk, n, distance):
        for c in range(2):
            home = homes[chunk][c]
            if distance < home:

                @pl.when(g == distance)
                def _():
                    add_in(True, chunk, c, n)
                    sum_copy(True, chunk, c, n).start()

            if last - distance > home:

                @pl.when(g == last - distance)
                def _():
                    add_in(False, chunk, c, n)
                    sum_copy(False, chunk, c, n).start()

    def out_copies(n, local):
        side, start = divmod(n * span, feats)
        made = []
        for kind, ref in enumerate((out_main, out_tangent)):
            dst = ref.at[pl.ds(pl.multiple_of(x * half, half), half), pl.ds(start, span)]
            if local:
                made.append(pltpu.make_async_copy(fin.at[n, kind], dst, out_sem.at[n, kind]))
            else:
                made.append(remote(fin.at[n, kind], dst, out_send.at[n, kind], out_recv.at[n, kind], twin))
        return side, made

    def sum_final(chunk, n):
        for c in range(2):
            home = homes[chunk][c]

            @pl.when(g == home)
            def _():
                total = part[chunk, c, n].astype(jnp.float32)
                for way, needed in ((0, home > 0), (1, home < last)):
                    if needed:
                        sum_copy(way == 0, chunk, c, n).wait_recv()
                        total = total + arrived[way, chunk, c, n].astype(jnp.float32)
                for kind in range(2):
                    at = (kind * 2 + c) * half
                    for m in range(span // width):
                        s = (n * span % feats) // width + m
                        fin[n, kind, :, m * width : (m + 1) * width] = (
                            gat[chunk, s, n * span // feats, kind, c].astype(jnp.float32)
                            + total[kind, :, m * width : (m + 1) * width]
                        ).astype(jnp.bfloat16)
                side, local = out_copies(n, True)
                _, far = out_copies(n, False)

                @pl.when(x == side)
                def _():
                    for copy in local:
                        copy.start()

                @pl.when(x != side)
                def _():
                    for copy in far:
                        copy.start()

    sends = (2, 0, 1)
    for j in range(8):
        for r in sends:
            z_start(r, j)

    @pl.when((g > 0) & (g < last))
    def _():
        for p in range(cuts):
            for r in sends:
                wz_start(r, p).start()

    locals_ = [pltpu.make_async_copy(piece(j, g), slot(j, g), own_sem.at[j]) for j in range(8)]
    for copy in locals_:
        copy.start()
    w_locals = [
        pltpu.make_async_copy(w_in_piece(g, p), w_in_slot(x, i, (g, p)), w_sem.at[p])
        for p in range(cuts)
    ] + [pltpu.make_async_copy(w_out, wol.at[x, i], w_sem.at[cuts])]
    for copy in w_locals:
        copy.start()
    for j in range(4):
        locals_[j].wait()
        kv_spread(3, j)
    go_start(0, 0, w_out_piece(0))

    def take(*which):
        for r, j in which:
            z_wait(r, j)
            kv_spread(r, j)

    take((2, 0), (0, 0), (2, 1), (0, 1), (1, 0))
    go_start(1, 1, w_out_piece(1))
    for j in range(4):
        kv_forward(3, j)
    go_first(0, 0)
    take((2, 2), (0, 2), (2, 3), (0, 3))
    go_start(2, 2, w_out_piece(2))
    for r, j in ((2, 0), (0, 0), (2, 1), (0, 1), (1, 0)):
        kv_forward(r, j)
    go_first(1, 1)
    take((1, 1))
    go_start(3, 3, w_out_piece(3))
    for r, j in ((2, 2), (0, 2), (2, 3), (0, 3), (1, 1)):
        kv_forward(r, j)
    w_out_rest(0)
    take((1, 2))
    for p in range(cuts):
        gi_start((g, p), (3, p), w_in_piece(g, p))
    go_first(2, 2)
    w_out_rest(1)
    take((1, 3))
    kv_forward(1, 2)
    go_first(3, 3)
    w_out_rest(2)
    kv_forward(1, 3)
    w_out_rest(3)
    for p in range(cuts):
        w_in_first(3, p)
    for j in range(4):
        for r in range(groups):
            kv_finish(r, j)
    for j in range(4, 8):
        locals_[j].wait()
        for r in (2, 0, 1):
            z_wait(r, j)

    @pl.when((g == 0) | (g == last))
    def _():
        for p in range(cuts):
            for r in sends:
                wz_start(r, p).start()

    for h in range(heads):
        attend_head(0, h)
    for p in range(cuts):
        w_in_rest(3, p)
    swap_start(0)
    line_step(0, 0, 0)
    w_in_start(2, 0)
    attend_head(1, 0)
    w_in_start(2, 1)
    w_in_first(2, 0)
    line_step(0, 1, 0)
    attend_head(1, 1)
    w_in_start(0, 0)
    w_in_rest(2, 0)
    w_in_first(2, 1)
    attend_head(1, 2)
    swap_start(1)
    w_in_start(1, 0)
    w_in_first(0, 0)
    w_in_rest(2, 1)
    line_step(0, 0, 1)
    w_in_first(1, 0)
    w_in_rest(0, 0)
    line_step(0, 1, 1)
    w_in_start(0, 1)
    w_in_rest(1, 0)
    line_step(0, 0, 2)
    w_in_first(0, 1)
    line_step(0, 1, 2)
    w_in_start(1, 1)
    w_in_rest(0, 1)
    line_step(1, 0, 0)
    line_step(1, 1, 0)
    w_in_first(1, 1)
    w_in_rest(1, 1)
    for copy in w_locals:
        copy.wait()
    for p in range(cuts):
        for r in range(groups):
            gi_finish((ranks[r], p), (r, p))
    line_step(0, 0, 3)
    line_step(0, 1, 3)
    mine[0].wait()
    hidden_left(0)
    tiles = hid.shape[1] // HIDDEN_TILE
    for n in range(tiles):
        hidden_tile(n)
        if n == tiles // 2:
            line_step(1, 0, 1)
            line_step(1, 1, 1)
    for r in range(parts):
        go_finish(r, r)
    pairs = slices // 2
    order = [m for both in zip(range(pairs // 2), range(pairs // 2, pairs)) for m in both]
    order_n = [2 * m + n for m in order for n in range(2)]
    for at, m in enumerate(order):
        out_slices(0, m)
        for n in range(2):
            sum_start(0, 2 * m + n, 2)
        if at == pairs // 2:
            line_step(1, 0, 2)
            line_step(1, 1, 2)
    for n in order_n:
        sum_start(0, n, 1)
    for n in order_n:
        sum_step(0, n, 1)
    line_step(1, 0, 3)
    line_step(1, 1, 3)
    mine[1].wait()
    hidden_left(1)
    for n in range(tiles):
        hidden_tile(n)
    for m in order:
        out_slices(1, m)
        for n in range(2):
            sum_start(1, 2 * m + n, 3)
    for n in order_n:
        sum_final(0, n)
    for at in range(slices + 2):
        if at < slices:
            sum_step(1, order_n[at], 1)
        if 0 < at <= slices:
            sum_step(1, order_n[at - 1], 2)
        if at > 1:
            sum_final(1, order_n[at - 2])
    for n in range(slices):
        side, local = out_copies(n, True)
        _, far = out_copies(n, False)

        @pl.when(x == side)
        def _():
            for copy in local:
                copy.wait()
            for copy in far:
                copy.wait_recv()

        @pl.when(x != side)
        def _():
            for copy in far:
                copy.wait_send()

    for copy in sent:
        copy.wait_send()
    for p in range(cuts):
        for r in range(last):
            wz_start(r, p).wait_send()
    for chunk in range(2):
        line_sent(chunk)
        for c in range(2):
            home = homes[chunk][c]
            for n in range(slices):

                @pl.when(g < home)
                def _():
                    sum_copy(True, chunk, c, n).wait_send()

                @pl.when(g > home)
                def _():
                    sum_copy(False, chunk, c, n).wait_send()


SLICES = 8
PARTS = 4
CUTS = 2
HIDDEN_TILE = 256


def by_layers(query, key, value, d_query, d_key, d_value, residual, d_residual, w_in, w_out, dp, seq):
    groups = seq // INNER
    rows, feats = query.shape
    half, width = rows // dp, feats // groups
    deep, hidden = w_in.shape[0], w_in.shape[1] // groups
    whole = dp * feats
    span = whole // SLICES
    dma = pltpu.SemaphoreType.DMA
    low = jnp.bfloat16
    last = groups - 1
    length = groups * INNER * rows
    flops = 12 * groups * rows * length * width + 8 * dp * hidden * whole * groups * half * 2
    return tuple(pl.pallas_call(
        block_kernel,
        in_specs=[pl.BlockSpec(memory_space=pl.ANY)] * 10,
        out_specs=[pl.BlockSpec(memory_space=pl.ANY)] * 2,
        out_shape=[jax.ShapeDtypeStruct((rows, feats), low)] * 2,
        scratch_shapes=[
            pltpu.VMEM((4, groups, rows, width), low),
            pltpu.VMEM((INNER, groups, 4, rows, width), low),
            pltpu.VMEM((groups, INNER, deep, dp * hidden), low),
            pltpu.VMEM((dp, INNER, w_out.shape[0], whole), low),
            pltpu.VMEM((dp, 2, 2, 2, half, width), low),
            pltpu.VMEM((2, groups, dp, 2, 2, half, width), low),
            pltpu.VMEM((4 * half, whole), low),
            pltpu.VMEM((4 * half, dp * hidden), low),
            pltpu.VMEM((2, 2, SLICES, 2, half, span), low),
            pltpu.VMEM((2, 2, 2, SLICES, 2, half, span), low),
            pltpu.VMEM((SLICES, 2, half, span), low),
            dma((last, 8)), dma((groups, 8)), dma((8,)),
        ]
        + [dma((groups, 4)) for _ in range(6)]
        + [dma((last, CUTS)), dma((groups, CUTS)), dma((groups, CUTS, 7)), dma((groups, CUTS, 7))]
        + [dma((PARTS, 7)), dma((PARTS, 7)), dma((CUTS + 1,))]
        + [dma((2,)), dma((2,)), dma((2,))]
        + [dma((2, 2, last)) for _ in range(4)]
        + [dma((2, 2, 2, SLICES)), dma((2, 2, 2, SLICES))]
        + [dma((SLICES, 2)) for _ in range(3)],
        cost_estimate=pl.CostEstimate(flops=flops, bytes_accessed=10**8, transcendentals=0),
        compiler_params=pltpu.CompilerParams(
            collective_id=0, has_side_effects=True, vmem_limit_bytes=60 * 2**20
        ),
        name="block",
    )(query, d_query, residual, d_residual, key, value, d_key, d_value, w_in, w_out))


def on_device(*args, dp, seq):
    query, w_in = args[0], args[8]
    groups = seq // INNER
    tile = groups * HEAD_DIM
    if dp != 2 or seq % INNER or groups != 4 or query.shape[1] % tile or w_in.shape[1] % tile:
        return by_rows(*args)
    return by_layers(*args, dp=dp, seq=seq)


def solution(mesh):
    in_specs = (P("seq", "dp"),) * 9 + (P(("dp", "seq"), None),)
    out_specs = (P("seq", "dp"), P("seq", "dp"))
    body = functools.partial(on_device, dp=mesh.shape["dp"], seq=mesh.shape["seq"])
    return jax.shard_map(
        body, mesh=mesh, in_specs=in_specs, out_specs=out_specs, check_vma=False
    )
```

```python
import functools
import math

import jax
import jax.numpy as jnp
from jax import lax
from jax.experimental import pallas as pl
from jax.experimental.pallas import tpu as pltpu
from jax.sharding import PartitionSpec as P

HEAD_DIM = 128


gelu_coeff = 0.7978845608
cubic_coeff = 0.044715


def gelu_pair(pre_act, d_pre_act):
    inner_arg = gelu_coeff * (pre_act + cubic_coeff * pre_act * pre_act * pre_act)
    hyper = jnp.tanh(inner_arg)
    gelu_value = 0.5 * pre_act * (1.0 + hyper)
    gelu_slope = 0.5 * (1.0 + hyper) + 0.5 * pre_act * (1.0 - hyper * hyper) * gelu_coeff * (
        1.0 + 3.0 * cubic_coeff * pre_act * pre_act
    )
    return (gelu_value, gelu_slope * d_pre_act)


def nt(a, b):
    return lax.dot_general(a, b, (((1,), (1,)), ((), ())), preferred_element_type=jnp.float32)


def attend_math(q, dq, res, dres, keys, values, keys_pair, values_pair):
    scale = 1.0 / math.sqrt(HEAD_DIM)
    scores = nt(q, keys) * scale
    d_scores = nt(jnp.concatenate([dq, q], axis=1), keys_pair) * scale
    peak = jnp.max(scores, axis=1, keepdims=True)
    weights = jnp.exp(scores - peak)
    mixed = weights * d_scores
    total = jnp.sum(weights, axis=1, keepdims=True)
    slope = jnp.sum(mixed, axis=1, keepdims=True)
    both = jnp.dot(weights.astype(jnp.bfloat16), values_pair, preferred_element_type=jnp.float32)
    tangent = both[:, HEAD_DIM:] + jnp.dot(
        mixed.astype(jnp.bfloat16), values, preferred_element_type=jnp.float32
    )
    attended = both[:, :HEAD_DIM] / total
    d_attended = tangent / total - (slope / total) * attended
    return (
        (res.astype(jnp.float32) + attended).astype(jnp.bfloat16),
        (dres.astype(jnp.float32) + d_attended).astype(jnp.bfloat16),
    )


def attend_kernel(q, dq, res, dres, k, v, dk, dv, out, *, rows):
    keys, values = k[...], v[...]
    keys_pair = jnp.concatenate([keys, dk[...]], axis=1)
    values_pair = jnp.concatenate([values, dv[...]], axis=1)
    for start in range(0, q.shape[0], rows):
        part = pl.ds(start, rows)
        out[0, part, :], out[1, part, :] = attend_math(
            q[part, :], dq[part, :], res[part, :], dres[part, :],
            keys, values, keys_pair, values_pair,
        )


def attend(query, d_query, residual, d_residual, kv):
    rows, feats = query.shape
    heads = feats // HEAD_DIM
    length = kv.shape[0]
    own = pl.BlockSpec((rows, HEAD_DIM), lambda h: (0, h))

    def kv_spec(i):
        return pl.BlockSpec((length, HEAD_DIM), lambda h: (0, i * heads + h))

    return pl.pallas_call(
        functools.partial(attend_kernel, rows=min(rows, 128)),
        grid=(heads,),
        in_specs=[own] * 4 + [kv_spec(i) for i in range(4)],
        out_specs=pl.BlockSpec((2, rows, HEAD_DIM), lambda h: (0, 0, h)),
        out_shape=jax.ShapeDtypeStruct((2, rows, feats), jnp.bfloat16),
        cost_estimate=pl.CostEstimate(
            flops=12 * rows * length * feats, bytes_accessed=8 * length * feats, transcendentals=0
        ),
        name="attend",
    )(query, d_query, residual, d_residual, kv, kv, kv, kv)


def by_rows(query, key, value, d_query, d_key, d_value, residual, d_residual, w_in, w_out):
    rows, feats = query.shape
    kv = lax.all_gather(
        jnp.concatenate([key, value, d_key, d_value], axis=1), "seq", axis=0, tiled=True
    )
    w_in_whole = lax.all_gather(w_in, "seq", axis=0, tiled=True)
    w_out_whole = lax.all_gather(w_out, "seq", axis=0, tiled=True)
    mixed = attend(query, d_query, residual, d_residual, kv).reshape(2 * rows, feats)
    whole = lax.all_gather(mixed, "dp", axis=1, tiled=True)
    pre = jnp.dot(whole, w_in_whole, preferred_element_type=jnp.float32)
    hidden, d_hidden = gelu_pair(pre[:rows], pre[rows:])
    hidden = jnp.concatenate([hidden.astype(jnp.bfloat16), d_hidden.astype(jnp.bfloat16)], axis=0)
    partial = jnp.dot(hidden, w_out_whole, preferred_element_type=jnp.float32)
    summed = lax.psum_scatter(
        partial.astype(jnp.bfloat16), "dp", scatter_dimension=1, tiled=True
    ).astype(jnp.float32)
    out = (mixed.astype(jnp.float32) + summed).astype(jnp.bfloat16)
    return (out[:rows], out[rows:])


INNER = 4
MESH = pl.DeviceIdType.MESH
COMM_COST = pl.CostEstimate(flops=10**11, bytes_accessed=10**8, transcendentals=0)


def place(groups):
    seq = lax.axis_index("seq")
    return lax.axis_index("dp"), lax.div(seq, INNER), lax.rem(seq, INNER)


def enter(devices):
    barrier = pltpu.get_barrier_semaphore()
    for device in devices:
        pl.semaphore_signal(barrier, inc=1, device_id=device, device_id_type=MESH)
    pl.semaphore_wait(barrier, len(devices))


def block_kernel(
    q, dq, res, dres, k, v, dk, dv, w_in, w_out, out_main, out_tangent,
    own, kv, wl, wol, mix, gat, left, hid, part, arrived, fin,
    z_send, z_recv, own_sem, ky_send, ky_recv, kp_send, kp_recv, kf_send, kf_recv,
    wz_send, wz_recv, gi_send, gi_recv, go_send, go_recv, w_sem,
    swap_send, swap_recv, mine_sem, right_send, right_recv, left_send, left_recv,
    rs_send, rs_recv, out_send, out_recv, out_sem,
):
    groups, width = own.shape[1], own.shape[3]
    feats = q.shape[1]
    hidden = w_in.shape[1] // groups
    heads = width // HEAD_DIM
    half = mix.shape[4]
    last = groups - 1
    slices = fin.shape[0]
    span = fin.shape[3]
    parts = go_send.shape[0]
    wide_out = w_out.shape[1] // parts
    cuts = wz_send.shape[1]
    deep_in = w_in.shape[0] // cuts
    homes = ((1, 2), (0, 3))
    x, g, i = place(groups)
    other = 1 - x
    core = lax.rem(i, 2)
    next_i = i + 1 - 2 * core
    across_i = lax.rem(i + 2, INNER)
    partner = (x, g * INNER + next_i)
    across = (x, g * INNER + across_i)
    twin = (other, g * INNER + i)
    high = lax.div(g, 2)
    ranks = (last * (1 - high), 2 - high, g + 1 - 2 * lax.rem(g, 2), g)
    peers = [(x, to * INNER + i) for to in ranks[:last]]
    up = (x, jnp.minimum(g + 1, last) * INNER + i)
    down = (x, jnp.maximum(g - 1, 0) * INNER + i)
    enter(peers + [partner, across, twin])

    def remote(src, dst, send, recv, device):
        return pltpu.make_async_remote_copy(
            src_ref=src, dst_ref=dst, send_sem=send, recv_sem=recv,
            device_id=device, device_id_type=MESH,
        )

    sent = []

    def go(copy):
        copy.start()
        sent.append(copy)
        return copy

    def piece(j, to):
        ref = (k, v, dk, dv, q, dq, res, dres)[j]
        return ref.at[:, pl.ds(pl.multiple_of(to * width, 128), width)]

    def slot(j, source):
        return kv.at[i, source, j] if j < 4 else own.at[j - 4, source]

    def z_start(r, j):
        go(remote(piece(j, ranks[r]), slot(j, g), z_send.at[r, j], z_recv.at[g, j], peers[r]))

    def z_wait(r, j):
        source = ranks[r]
        remote(piece(j, source), slot(j, source), z_send.at[r, j], z_recv.at[source, j], peers[r]).wait_recv()

    def w_in_piece(to, p):
        return w_in.at[pl.ds(p * deep_in, deep_in), pl.ds(pl.multiple_of(to * hidden, 128), hidden)]

    def w_in_slot(xs, at, n):
        s, p = n
        columns = pl.ds(pl.multiple_of(xs * hidden, 128), hidden)
        return wl.at[s, at, pl.ds(p * deep_in, deep_in), columns]

    def w_out_piece(r):
        return w_out.at[:, pl.ds(r * wide_out, wide_out)]

    def w_out_slot(xs, at, r):
        return wol.at[xs, at, :, pl.ds(r * wide_out, wide_out)]

    def gather(slot_of, send, recv, first, second, first_at, second_at):
        def copy(which, src_at, n, idx, device, src=None):
            dst = slot_of(src_at[0], src_at[1], n)
            at = idx if isinstance(idx, tuple) else (idx,)
            return remote(src if src is not None else dst, dst,
                          send.at[at + (which,)], recv.at[at + (which,)], device)

        def start(n, idx, src=None, which=(0, 1, 2)):
            for to in which:
                go(copy(to, (x, i), n, idx, (first, second, partner)[to], src))

        def wait(which, at, n, idx):
            copy(which, at, n, idx, partner).wait_recv()

        def from_first(n, idx):
            wait(0, first_at, n, idx)
            go(copy(3, first_at, n, idx, second))
            go(copy(4, first_at, n, idx, partner))

        def from_second(n, idx):
            wait(1, second_at, n, idx)
            go(copy(5, second_at, n, idx, partner))

        def from_far(n, idx):
            far = (other, across_i)
            wait(3, far, n, idx)
            go(copy(6, far, n, idx, partner))

        def finish(n, idx):
            for which, at in ((2, (x, i)), (4, first_at), (5, second_at), (6, (other, across_i))):
                wait(which, (at[0], at[1] + 1 - 2 * lax.rem(at[1], 2)), n, idx)

        return start, from_first, from_second, from_far, finish

    def pick(a, b):
        return tuple(jnp.where(core == 0, m, n) for m, n in zip(a, b))

    go_start, go_first, go_second, go_far, go_finish = gather(
        w_out_slot, go_send, go_recv, across, twin, (x, across_i), (other, i),
    )
    gi_start, gi_first, gi_second, gi_far, gi_finish = gather(
        w_in_slot, gi_send, gi_recv, pick(twin, across), pick(across, twin),
        pick((other, i), (x, across_i)), pick((x, across_i), (other, i)),
    )

    def wz_start(r, p):
        return remote(
            w_in_piece(ranks[r], p), w_in_slot(x, i, (g, p)),
            wz_send.at[r, p], wz_recv.at[g, p], peers[r],
        )

    def w_in_first(t, p):
        gi_first((ranks[t], p), (t, p))

    def w_in_rest(t, p):
        gi_second((ranks[t], p), (t, p))
        gi_far((ranks[t], p), (t, p))

    def w_in_start(t, p):
        source = ranks[t]
        remote(
            w_in_piece(source, p), w_in_slot(x, i, (source, p)),
            wz_send.at[t, p], wz_recv.at[source, p], peers[t],
        ).wait_recv()
        gi_start((ranks[t], p), (t, p))

    def w_out_rest(r):
        go_second(r, r)
        go_far(r, r)

    def kv_copy(at, t, j, send, recv, device):
        block = kv.at[at, ranks[t], j]
        return remote(block, block, send.at[t, j], recv.at[t, j], device)

    def kv_spread(t, j):
        go(kv_copy(i, t, j, ky_send, ky_recv, across))
        go(kv_copy(i, t, j, kp_send, kp_recv, partner))

    def kv_forward(t, j):
        kv_copy(across_i, t, j, ky_send, ky_recv, across).wait_recv()
        go(kv_copy(across_i, t, j, kf_send, kf_recv, partner))

    def kv_finish(t, j):
        kv_copy(next_i, t, j, kp_send, kp_recv, partner).wait_recv()
        at = across_i + 1 - 2 * lax.rem(across_i, 2)
        kv_copy(at, t, j, kf_send, kf_recv, partner).wait_recv()

    def attend_head(chunk, h):
        feat = pl.ds(h * HEAD_DIM, HEAD_DIM)
        length = kv.shape[0] * kv.shape[1] * kv.shape[3]
        keys, values, d_keys, d_values = (
            kv[:, :, j, :, feat].reshape(length, HEAD_DIM) for j in range(4)
        )
        keys_pair = jnp.concatenate([keys, d_keys], axis=1)
        values_pair = jnp.concatenate([values, d_values], axis=1)
        for c in range(2):
            home = homes[chunk][c]
            pair = attend_math(
                own[0, home, :, feat], own[1, home, :, feat],
                own[2, home, :, feat], own[3, home, :, feat],
                keys, values, keys_pair, values_pair,
            )
            for side in range(2):
                for kind in range(2):
                    mix[side, chunk, kind, c, :, feat] = pair[kind][side * half : (side + 1) * half]

    def swap(chunk):
        return remote(mix.at[other, chunk], gat.at[chunk, g, x],
                      swap_send.at[chunk], swap_recv.at[chunk], twin)

    def hop(chunk, c, t, to_right):
        source = g - t if to_right else g + t
        sends, recvs = (right_send, right_recv) if to_right else (left_send, left_recv)
        side = other if c else x
        return remote(
            mix.at[x, chunk] if c == 0 and t == 0 else gat.at[chunk, source, side],
            gat.at[chunk, source, side],
            sends.at[chunk, c, t], recvs.at[chunk, c, t], up if to_right else down,
        )

    def sends_right(t):
        return (g >= t) & (g < last)

    def sends_left(t):
        return (g + t <= last) & (g > 0)

    def line_step(chunk, c, t):
        if t == 0 and c:
            swap(chunk).wait_recv()
        for to_right, sends in ((True, sends_right), (False, sends_left)):

            @pl.when(sends(t))
            def _():
                if t:
                    hop(chunk, c, t - 1, to_right).wait_recv()
                hop(chunk, c, t, to_right).start()

    def line_finish(chunk, c):
        for to_right, end in ((True, last), (False, 0)):

            @pl.when(g == end)
            def _():
                for t in range(last):
                    hop(chunk, c, t, to_right).wait_recv()

    mine = {}

    def swap_start(chunk):
        go(swap(chunk))
        mine[chunk] = pltpu.make_async_copy(mix.at[x, chunk], gat.at[chunk, g, x], mine_sem.at[chunk])
        mine[chunk].start()

    def line_sent(chunk):
        for c in range(2):
            for t in range(last):

                @pl.when(sends_right(t))
                def _():
                    hop(chunk, c, t, True).wait_send()

                @pl.when(sends_left(t))
                def _():
                    hop(chunk, c, t, False).wait_send()

    def hidden_left(chunk):
        for xs in range(2):
            for s in range(groups):
                start = (xs * groups + s) * width
                left[:, start : start + width] = gat[chunk, s, xs].reshape(hid.shape[0], width)

    def hidden_tile(n):
        rows, tile = hid.shape[0], HIDDEN_TILE
        columns = slice(n * tile, (n + 1) * tile)
        total = jnp.dot(
            left[...], wl[:, :, :, columns].reshape(left.shape[1], tile),
            preferred_element_type=jnp.float32,
        )
        value, tangent = gelu_pair(total[: rows // 2], total[rows // 2 :])
        hid[: rows // 2, columns] = value.astype(jnp.bfloat16)
        hid[rows // 2 :, columns] = tangent.astype(jnp.bfloat16)

    def out_slices(chunk, m):
        wide = 2 * span
        total = jnp.dot(
            hid[...], wol[:, :, :, m * wide : (m + 1) * wide].reshape(hid.shape[1], wide),
            preferred_element_type=jnp.float32,
        ).astype(jnp.bfloat16)
        for kind in range(2):
            for c in range(2):
                at = (kind * 2 + c) * half
                for n in range(2):
                    part[chunk, c, 2 * m + n, kind] = total[at : at + half, n * span : (n + 1) * span]

    def sum_copy(to_up, chunk, c, n):
        way = 0 if to_up else 1
        return remote(
            part.at[chunk, c, n], arrived.at[way, chunk, c, n],
            rs_send.at[way, chunk, c, n], rs_recv.at[way, chunk, c, n], up if to_up else down,
        )

    def add_in(to_up, chunk, c, n):
        sum_copy(to_up, chunk, c, n).wait_recv()
        way = 0 if to_up else 1
        part[chunk, c, n] = (
            part[chunk, c, n].astype(jnp.float32) + arrived[way, chunk, c, n].astype(jnp.float32)
        ).astype(jnp.bfloat16)

    def sum_start(chunk, n, distance):
        for c in range(2):
            home = homes[chunk][c]
            if home == distance:

                @pl.when(g == 0)
                def _():
                    sum_copy(True, chunk, c, n).start()

            if home == last - distance:

                @pl.when(g == last)
                def _():
                    sum_copy(False, chunk, c, n).start()

    def sum_step(chunk, n, distance):
        for c in range(2):
            home = homes[chunk][c]
            if distance < home:

                @pl.when(g == distance)
                def _():
                    add_in(True, chunk, c, n)
                    sum_copy(True, chunk, c, n).start()

            if last - distance > home:

                @pl.when(g == last - distance)
                def _():
                    add_in(False, chunk, c, n)
                    sum_copy(False, chunk, c, n).start()

    def out_copies(n, local):
        side, start = divmod(n * span, feats)
        made = []
        for kind, ref in enumerate((out_main, out_tangent)):
            dst = ref.at[pl.ds(pl.multiple_of(x * half, half), half), pl.ds(start, span)]
            if local:
                made.append(pltpu.make_async_copy(fin.at[n, kind], dst, out_sem.at[n, kind]))
            else:
                made.append(remote(fin.at[n, kind], dst, out_send.at[n, kind], out_recv.at[n, kind], twin))
        return side, made

    def sum_final(chunk, n):
        for c in range(2):
            home = homes[chunk][c]

            @pl.when(g == home)
            def _():
                total = part[chunk, c, n].astype(jnp.float32)
                for way, needed in ((0, home > 0), (1, home < last)):
                    if needed:
                        sum_copy(way == 0, chunk, c, n).wait_recv()
                        total = total + arrived[way, chunk, c, n].astype(jnp.float32)
                for kind in range(2):
                    at = (kind * 2 + c) * half
                    for m in range(span // width):
                        s = (n * span % feats) // width + m
                        fin[n, kind, :, m * width : (m + 1) * width] = (
                            gat[chunk, s, n * span // feats, kind, c].astype(jnp.float32)
                            + total[kind, :, m * width : (m + 1) * width]
                        ).astype(jnp.bfloat16)
                side, local = out_copies(n, True)
                _, far = out_copies(n, False)

                @pl.when(x == side)
                def _():
                    for copy in local:
                        copy.start()

                @pl.when(x != side)
                def _():
                    for copy in far:
                        copy.start()

    sends = (2, 0, 1)
    w_in_first_pieces = ((2, 0), (2, 1), (0, 0), (1, 0))
    w_in_last_pieces = ((0, 1), (1, 1))
    inner = (g > 0) & (g < last)
    outer = (g == 0) | (g == last)

    def w_in_send(pieces):
        for r, p in pieces:
            wz_start(r, p).start()

    for j in range(8):
        for r in sends:
            z_start(r, j)

    @pl.when(inner)
    def _():
        w_in_send(w_in_first_pieces)

    locals_ = [pltpu.make_async_copy(piece(j, g), slot(j, g), own_sem.at[j]) for j in range(8)]
    for copy in locals_:
        copy.start()
    w_locals = [
        pltpu.make_async_copy(w_in_piece(g, p), w_in_slot(x, i, (g, p)), w_sem.at[p])
        for p in range(cuts)
    ] + [pltpu.make_async_copy(w_out, wol.at[x, i], w_sem.at[cuts])]
    for copy in w_locals:
        copy.start()
    for j in range(4):
        locals_[j].wait()
        kv_spread(3, j)
    for p in range(cuts):
        gi_start((g, p), (3, p), w_in_piece(g, p))
    for r in range(parts - 1):
        go_start(r, r, w_out_piece(r), (1,))

    def take(*which):
        for r, j in which:
            z_wait(r, j)
            kv_spread(r, j)

    def onward(*which):
        for r, j in which:
            kv_forward(r, j)

    def w_out_start(r):
        go_start(r, r, w_out_piece(r), (0, 2))

    take((2, 0), (0, 0))
    w_out_start(0)
    take((2, 1), (0, 1), (1, 0))
    onward((3, 0), (3, 1), (3, 2), (3, 3))
    for p in range(cuts):
        w_in_first(3, p)
    take((2, 2), (0, 2), (2, 3), (0, 3))
    w_out_start(1)
    for p in range(cuts):
        w_in_rest(3, p)
    onward((2, 0), (0, 0), (2, 1), (0, 1), (1, 0))
    go_first(0, 0)
    take((1, 1))
    w_out_start(2)
    onward((2, 2), (0, 2), (2, 3), (0, 3))
    w_out_rest(0)
    take((1, 2))
    onward((1, 1))
    go_first(1, 1)
    take((1, 3))
    go_first(2, 2)
    w_out_rest(1)
    onward((1, 2), (1, 3))
    w_out_rest(2)
    for j in range(4, 8):
        locals_[j].wait()
        for r in (2, 0, 1):
            z_wait(r, j)
        if j == 6:


            @pl.when(outer)
            def _():
                w_in_send(w_in_first_pieces)

    for j in range(4):
        for r in range(groups):
            kv_finish(r, j)
    attend_head(0, 0)
    w_in_start(2, 0)
    attend_head(0, 1)
    attend_head(0, 2)
    swap_start(0)
    line_step(0, 0, 0)
    w_in_start(2, 1)
    w_in_first(2, 0)
    attend_head(1, 0)
    w_in_start(1, 0)
    line_step(0, 1, 0)
    w_in_send(w_in_last_pieces)
    w_in_rest(2, 0)
    w_in_first(2, 1)
    attend_head(1, 1)
    w_in_rest(2, 1)
    w_in_first(1, 0)
    attend_head(1, 2)
    w_in_start(0, 0)
    line_step(0, 0, 1)
    w_in_rest(1, 0)
    w_in_first(0, 0)
    line_step(0, 1, 1)
    w_in_rest(0, 0)
    line_step(0, 0, 2)
    w_in_start(1, 1)
    w_in_start(0, 1)
    line_step(0, 1, 2)
    line_step(1, 0, 0)
    w_in_first(1, 1)
    w_in_first(0, 1)
    swap_start(1)
    w_in_rest(1, 1)
    go_start(3, 3, w_out_piece(3))
    w_in_rest(0, 1)
    line_step(1, 1, 0)
    line_step(1, 0, 1)
    for copy in w_locals:
        copy.wait()
    for p in range(cuts):
        for r in range(groups):
            gi_finish((ranks[r], p), (r, p))
    line_finish(0, 0)
    line_finish(0, 1)
    mine[0].wait()
    hidden_left(0)
    tiles = hid.shape[1] // HIDDEN_TILE
    for n in range(tiles):
        hidden_tile(n)
        if n == 2:
            line_step(1, 1, 1)
        if n == 4:
            go_first(3, 3)
            line_step(1, 0, 2)
    for r in range(parts - 1):
        go_finish(r, r)
    pairs = slices // 2
    order = [m for both in zip(range(pairs // 2), range(pairs // 2, pairs)) for m in both]
    order_n = [2 * m + n for m in order for n in range(2)]
    for m in order:
        if m == order[-1]:
            w_out_rest(3)
            go_finish(3, 3)
        out_slices(0, m)
        for n in range(2):
            sum_start(0, 2 * m + n, 2)
    for n in order_n[:2]:
        sum_start(0, n, 1)
    line_step(1, 1, 2)
    for c in range(2):
        line_finish(1, c)
    mine[1].wait()
    hidden_left(1)
    waiting = list(order_n)
    for n in range(tiles):
        hidden_tile(n)
        if n % 2:
            sum_step(0, waiting.pop(0), 1)
    for m in order:
        out_slices(1, m)
        for n in range(2):
            sum_start(1, 2 * m + n, 3)
        sum_step(0, waiting.pop(0), 1)
    for n in waiting:
        sum_step(0, n, 1)
    for n in order_n[2:]:
        sum_start(0, n, 1)
    for at in range(slices + 2):
        if at < slices:
            sum_step(1, order_n[at], 1)
        if 0 < at <= slices:
            sum_step(1, order_n[at - 1], 2)
        if at > 1:
            sum_final(1, order_n[at - 2])
    for n in order_n:
        sum_final(0, n)
    for n in range(slices):
        side, local = out_copies(n, True)
        _, far = out_copies(n, False)

        @pl.when(x == side)
        def _():
            for copy in local:
                copy.wait()
            for copy in far:
                copy.wait_recv()

        @pl.when(x != side)
        def _():
            for copy in far:
                copy.wait_send()

    for copy in sent:
        copy.wait_send()
    for p in range(cuts):
        for r in range(last):
            wz_start(r, p).wait_send()
    for chunk in range(2):
        line_sent(chunk)
        for c in range(2):
            home = homes[chunk][c]
            for n in range(slices):

                @pl.when(g < home)
                def _():
                    sum_copy(True, chunk, c, n).wait_send()

                @pl.when(g > home)
                def _():
                    sum_copy(False, chunk, c, n).wait_send()


SLICES = 8
PARTS = 4
CUTS = 2
HIDDEN_TILE = 256


def by_layers(query, key, value, d_query, d_key, d_value, residual, d_residual, w_in, w_out, dp, seq):
    groups = seq // INNER
    rows, feats = query.shape
    half, width = rows // dp, feats // groups
    deep, hidden = w_in.shape[0], w_in.shape[1] // groups
    whole = dp * feats
    span = whole // SLICES
    dma = pltpu.SemaphoreType.DMA
    low = jnp.bfloat16
    last = groups - 1
    length = groups * INNER * rows
    flops = 12 * groups * rows * length * width + 8 * dp * hidden * whole * groups * half * 2
    return tuple(pl.pallas_call(
        block_kernel,
        in_specs=[pl.BlockSpec(memory_space=pl.ANY)] * 10,
        out_specs=[pl.BlockSpec(memory_space=pl.ANY)] * 2,
        out_shape=[jax.ShapeDtypeStruct((rows, feats), low)] * 2,
        scratch_shapes=[
            pltpu.VMEM((4, groups, rows, width), low),
            pltpu.VMEM((INNER, groups, 4, rows, width), low),
            pltpu.VMEM((groups, INNER, deep, dp * hidden), low),
            pltpu.VMEM((dp, INNER, w_out.shape[0], whole), low),
            pltpu.VMEM((dp, 2, 2, 2, half, width), low),
            pltpu.VMEM((2, groups, dp, 2, 2, half, width), low),
            pltpu.VMEM((4 * half, whole), low),
            pltpu.VMEM((4 * half, dp * hidden), low),
            pltpu.VMEM((2, 2, SLICES, 2, half, span), low),
            pltpu.VMEM((2, 2, 2, SLICES, 2, half, span), low),
            pltpu.VMEM((SLICES, 2, half, span), low),
            dma((last, 8)), dma((groups, 8)), dma((8,)),
        ]
        + [dma((groups, 4)) for _ in range(6)]
        + [dma((last, CUTS)), dma((groups, CUTS)), dma((groups, CUTS, 7)), dma((groups, CUTS, 7))]
        + [dma((PARTS, 7)), dma((PARTS, 7)), dma((CUTS + 1,))]
        + [dma((2,)), dma((2,)), dma((2,))]
        + [dma((2, 2, last)) for _ in range(4)]
        + [dma((2, 2, 2, SLICES)), dma((2, 2, 2, SLICES))]
        + [dma((SLICES, 2)) for _ in range(3)],
        cost_estimate=pl.CostEstimate(flops=flops, bytes_accessed=10**8, transcendentals=0),
        compiler_params=pltpu.CompilerParams(
            collective_id=0, has_side_effects=True, vmem_limit_bytes=60 * 2**20
        ),
        name="block",
    )(query, d_query, residual, d_residual, key, value, d_key, d_value, w_in, w_out))


def on_device(*args, dp, seq):
    query, w_in = args[0], args[8]
    groups = seq // INNER
    tile = groups * HEAD_DIM
    if dp != 2 or seq % INNER or groups != 4 or query.shape[1] % tile or w_in.shape[1] % tile:
        return by_rows(*args)
    return by_layers(*args, dp=dp, seq=seq)


def solution(mesh):
    in_specs = (P("seq", "dp"),) * 9 + (P(("dp", "seq"), None),)
    out_specs = (P("seq", "dp"), P("seq", "dp"))
    body = functools.partial(on_device, dp=mesh.shape["dp"], seq=mesh.shape["seq"])
    return jax.shard_map(
        body, mesh=mesh, in_specs=in_specs, out_specs=out_specs, check_vma=False
    )
```

```python
import functools
import math

import jax
import jax.numpy as jnp
from jax import lax
from jax.experimental import pallas as pl
from jax.experimental.pallas import tpu as pltpu
from jax.sharding import PartitionSpec as P

HEAD_DIM = 128


gelu_coeff = 0.7978845608
cubic_coeff = 0.044715


def gelu_pair(pre_act, d_pre_act):
    inner_arg = gelu_coeff * (pre_act + cubic_coeff * pre_act * pre_act * pre_act)
    hyper = jnp.tanh(inner_arg)
    gelu_value = 0.5 * pre_act * (1.0 + hyper)
    gelu_slope = 0.5 * (1.0 + hyper) + 0.5 * pre_act * (1.0 - hyper * hyper) * gelu_coeff * (
        1.0 + 3.0 * cubic_coeff * pre_act * pre_act
    )
    return (gelu_value, gelu_slope * d_pre_act)


def nt(a, b):
    return lax.dot_general(a, b, (((1,), (1,)), ((), ())), preferred_element_type=jnp.float32)


def attend_math(q, dq, res, dres, keys, values, keys_pair, values_pair):
    scale = 1.0 / math.sqrt(HEAD_DIM)
    scores = nt(q, keys) * scale
    d_scores = nt(jnp.concatenate([dq, q], axis=1), keys_pair) * scale
    peak = jnp.max(scores, axis=1, keepdims=True)
    weights = jnp.exp(scores - peak)
    mixed = weights * d_scores
    total = jnp.sum(weights, axis=1, keepdims=True)
    slope = jnp.sum(mixed, axis=1, keepdims=True)
    both = jnp.dot(weights.astype(jnp.bfloat16), values_pair, preferred_element_type=jnp.float32)
    tangent = both[:, HEAD_DIM:] + jnp.dot(
        mixed.astype(jnp.bfloat16), values, preferred_element_type=jnp.float32
    )
    attended = both[:, :HEAD_DIM] / total
    d_attended = tangent / total - (slope / total) * attended
    return (
        (res.astype(jnp.float32) + attended).astype(jnp.bfloat16),
        (dres.astype(jnp.float32) + d_attended).astype(jnp.bfloat16),
    )


def attend_kernel(q, dq, res, dres, k, v, dk, dv, out, *, rows):
    keys, values = k[...], v[...]
    keys_pair = jnp.concatenate([keys, dk[...]], axis=1)
    values_pair = jnp.concatenate([values, dv[...]], axis=1)
    for start in range(0, q.shape[0], rows):
        part = pl.ds(start, rows)
        out[0, part, :], out[1, part, :] = attend_math(
            q[part, :], dq[part, :], res[part, :], dres[part, :],
            keys, values, keys_pair, values_pair,
        )


def attend(query, d_query, residual, d_residual, kv):
    rows, feats = query.shape
    heads = feats // HEAD_DIM
    length = kv.shape[0]
    own = pl.BlockSpec((rows, HEAD_DIM), lambda h: (0, h))

    def kv_spec(i):
        return pl.BlockSpec((length, HEAD_DIM), lambda h: (0, i * heads + h))

    return pl.pallas_call(
        functools.partial(attend_kernel, rows=min(rows, 128)),
        grid=(heads,),
        in_specs=[own] * 4 + [kv_spec(i) for i in range(4)],
        out_specs=pl.BlockSpec((2, rows, HEAD_DIM), lambda h: (0, 0, h)),
        out_shape=jax.ShapeDtypeStruct((2, rows, feats), jnp.bfloat16),
        cost_estimate=pl.CostEstimate(
            flops=12 * rows * length * feats, bytes_accessed=8 * length * feats, transcendentals=0
        ),
        name="attend",
    )(query, d_query, residual, d_residual, kv, kv, kv, kv)


def by_rows(query, key, value, d_query, d_key, d_value, residual, d_residual, w_in, w_out):
    rows, feats = query.shape
    kv = lax.all_gather(
        jnp.concatenate([key, value, d_key, d_value], axis=1), "seq", axis=0, tiled=True
    )
    w_in_whole = lax.all_gather(w_in, "seq", axis=0, tiled=True)
    w_out_whole = lax.all_gather(w_out, "seq", axis=0, tiled=True)
    mixed = attend(query, d_query, residual, d_residual, kv).reshape(2 * rows, feats)
    whole = lax.all_gather(mixed, "dp", axis=1, tiled=True)
    pre = jnp.dot(whole, w_in_whole, preferred_element_type=jnp.float32)
    hidden, d_hidden = gelu_pair(pre[:rows], pre[rows:])
    hidden = jnp.concatenate([hidden.astype(jnp.bfloat16), d_hidden.astype(jnp.bfloat16)], axis=0)
    partial = jnp.dot(hidden, w_out_whole, preferred_element_type=jnp.float32)
    summed = lax.psum_scatter(
        partial.astype(jnp.bfloat16), "dp", scatter_dimension=1, tiled=True
    ).astype(jnp.float32)
    out = (mixed.astype(jnp.float32) + summed).astype(jnp.bfloat16)
    return (out[:rows], out[rows:])


INNER = 4
MESH = pl.DeviceIdType.MESH
COMM_COST = pl.CostEstimate(flops=10**11, bytes_accessed=10**8, transcendentals=0)


def place(groups):
    seq = lax.axis_index("seq")
    return lax.axis_index("dp"), lax.div(seq, INNER), lax.rem(seq, INNER)


def enter(devices):
    barrier = pltpu.get_barrier_semaphore()
    for device in devices:
        pl.semaphore_signal(barrier, inc=1, device_id=device, device_id_type=MESH)
    pl.semaphore_wait(barrier, len(devices))


def block_kernel(
    q, dq, res, dres, k, v, dk, dv, w_in, w_out, out_main, out_tangent,
    own, kv, wl, wol, mix, gat, left, hid, part, arrived, fin,
    z_send, z_recv, own_sem, ky_send, ky_recv, kp_send, kp_recv, kf_send, kf_recv,
    wz_send, wz_recv, gi_send, gi_recv, go_send, go_recv, w_sem,
    swap_send, swap_recv, mine_sem, right_send, right_recv, left_send, left_recv,
    rs_send, rs_recv, out_send, out_recv, out_sem,
):
    groups, width = own.shape[1], own.shape[3]
    feats = q.shape[1]
    hidden = w_in.shape[1] // groups
    heads = width // HEAD_DIM
    half = mix.shape[4]
    last = groups - 1
    slices = fin.shape[0]
    span = fin.shape[3]
    parts = go_send.shape[0]
    wide_out = w_out.shape[1] // parts
    cuts = wz_send.shape[1]
    deep_in = w_in.shape[0] // cuts
    homes = ((1, 2), (0, 3))
    x, g, i = place(groups)
    other = 1 - x
    core = lax.rem(i, 2)
    next_i = i + 1 - 2 * core
    across_i = lax.rem(i + 2, INNER)
    partner = (x, g * INNER + next_i)
    across = (x, g * INNER + across_i)
    twin = (other, g * INNER + i)
    high = lax.div(g, 2)
    ranks = (last * (1 - high), 2 - high, g + 1 - 2 * lax.rem(g, 2), g)
    peers = [(x, to * INNER + i) for to in ranks[:last]]
    up = (x, jnp.minimum(g + 1, last) * INNER + i)
    down = (x, jnp.maximum(g - 1, 0) * INNER + i)
    enter(peers + [partner, across, twin])

    def remote(src, dst, send, recv, device):
        return pltpu.make_async_remote_copy(
            src_ref=src, dst_ref=dst, send_sem=send, recv_sem=recv,
            device_id=device, device_id_type=MESH,
        )

    sent = []

    def go(copy):
        copy.start()
        sent.append(copy)
        return copy

    def piece(j, to):
        ref = (k, v, dk, dv, q, dq, res, dres)[j]
        return ref.at[:, pl.ds(pl.multiple_of(to * width, 128), width)]

    def slot(j, source):
        return kv.at[i, source, j] if j < 4 else own.at[j - 4, source]

    def z_start(r, j):
        go(remote(piece(j, ranks[r]), slot(j, g), z_send.at[r, j], z_recv.at[g, j], peers[r]))

    def z_wait(r, j):
        source = ranks[r]
        remote(piece(j, source), slot(j, source), z_send.at[r, j], z_recv.at[source, j], peers[r]).wait_recv()

    def w_in_piece(to, p):
        return w_in.at[pl.ds(p * deep_in, deep_in), pl.ds(pl.multiple_of(to * hidden, 128), hidden)]

    def w_in_slot(xs, at, n):
        s, p = n
        columns = pl.ds(pl.multiple_of(xs * hidden, 128), hidden)
        return wl.at[s, at, pl.ds(p * deep_in, deep_in), columns]

    def w_out_piece(r):
        return w_out.at[:, pl.ds(r * wide_out, wide_out)]

    def w_out_slot(xs, at, r):
        return wol.at[xs, at, :, pl.ds(r * wide_out, wide_out)]

    def gather(slot_of, send, recv, first, second, first_at, second_at):
        def copy(which, src_at, n, idx, device, src=None):
            dst = slot_of(src_at[0], src_at[1], n)
            at = idx if isinstance(idx, tuple) else (idx,)
            return remote(src if src is not None else dst, dst,
                          send.at[at + (which,)], recv.at[at + (which,)], device)

        def start(n, idx, src=None, which=(0, 1, 2)):
            for to in which:
                go(copy(to, (x, i), n, idx, (first, second, partner)[to], src))

        def wait(which, at, n, idx):
            copy(which, at, n, idx, partner).wait_recv()

        def from_first(n, idx):
            wait(0, first_at, n, idx)
            go(copy(3, first_at, n, idx, second))
            go(copy(4, first_at, n, idx, partner))

        def from_second(n, idx):
            wait(1, second_at, n, idx)
            go(copy(5, second_at, n, idx, partner))

        def from_far(n, idx):
            far = (other, across_i)
            wait(3, far, n, idx)
            go(copy(6, far, n, idx, partner))

        def finish(n, idx):
            for which, at in ((2, (x, i)), (4, first_at), (5, second_at), (6, (other, across_i))):
                wait(which, (at[0], at[1] + 1 - 2 * lax.rem(at[1], 2)), n, idx)

        return start, from_first, from_second, from_far, finish

    def pick(a, b):
        return tuple(jnp.where(core == 0, m, n) for m, n in zip(a, b))

    go_start, go_first, go_second, go_far, go_finish = gather(
        w_out_slot, go_send, go_recv, across, twin, (x, across_i), (other, i),
    )
    gi_start, gi_first, gi_second, gi_far, gi_finish = gather(
        w_in_slot, gi_send, gi_recv, pick(twin, across), pick(across, twin),
        pick((other, i), (x, across_i)), pick((x, across_i), (other, i)),
    )

    def wz_start(r, p):
        return remote(
            w_in_piece(ranks[r], p), w_in_slot(x, i, (g, p)),
            wz_send.at[r, p], wz_recv.at[g, p], peers[r],
        )

    def w_in_first(t, p):
        gi_first((ranks[t], p), (t, p))

    def w_in_rest(t, p):
        gi_second((ranks[t], p), (t, p))
        gi_far((ranks[t], p), (t, p))

    def w_in_start(t, p):
        source = ranks[t]
        remote(
            w_in_piece(source, p), w_in_slot(x, i, (source, p)),
            wz_send.at[t, p], wz_recv.at[source, p], peers[t],
        ).wait_recv()
        gi_start((ranks[t], p), (t, p))

    def w_out_rest(r):
        go_second(r, r)
        go_far(r, r)

    def kv_copy(at, t, j, send, recv, device):
        block = kv.at[at, ranks[t], j]
        return remote(block, block, send.at[t, j], recv.at[t, j], device)

    def kv_spread(t, j):
        go(kv_copy(i, t, j, ky_send, ky_recv, across))
        go(kv_copy(i, t, j, kp_send, kp_recv, partner))

    def kv_forward(t, j):
        kv_copy(across_i, t, j, ky_send, ky_recv, across).wait_recv()
        go(kv_copy(across_i, t, j, kf_send, kf_recv, partner))

    def kv_finish(t, j):
        kv_copy(next_i, t, j, kp_send, kp_recv, partner).wait_recv()
        at = across_i + 1 - 2 * lax.rem(across_i, 2)
        kv_copy(at, t, j, kf_send, kf_recv, partner).wait_recv()

    def attend_head(chunk, h):
        feat = pl.ds(h * HEAD_DIM, HEAD_DIM)
        length = kv.shape[0] * kv.shape[1] * kv.shape[3]
        keys, values, d_keys, d_values = (
            kv[:, :, j, :, feat].reshape(length, HEAD_DIM) for j in range(4)
        )
        keys_pair = jnp.concatenate([keys, d_keys], axis=1)
        values_pair = jnp.concatenate([values, d_values], axis=1)
        for c in range(2):
            home = homes[chunk][c]
            pair = attend_math(
                own[0, home, :, feat], own[1, home, :, feat],
                own[2, home, :, feat], own[3, home, :, feat],
                keys, values, keys_pair, values_pair,
            )
            for side in range(2):
                for kind in range(2):
                    mix[side, chunk, kind, c, :, feat] = pair[kind][side * half : (side + 1) * half]

    def swap(chunk):
        return remote(mix.at[other, chunk], gat.at[chunk, g, x],
                      swap_send.at[chunk], swap_recv.at[chunk], twin)

    def hop(chunk, c, t, to_right):
        source = g - t if to_right else g + t
        sends, recvs = (right_send, right_recv) if to_right else (left_send, left_recv)
        side = other if c else x
        return remote(
            mix.at[x, chunk] if c == 0 and t == 0 else gat.at[chunk, source, side],
            gat.at[chunk, source, side],
            sends.at[chunk, c, t], recvs.at[chunk, c, t], up if to_right else down,
        )

    def sends_right(t):
        return (g >= t) & (g < last)

    def sends_left(t):
        return (g + t <= last) & (g > 0)

    def line_step(chunk, c, t):
        if t == 0 and c:
            swap(chunk).wait_recv()
        for to_right, sends in ((True, sends_right), (False, sends_left)):

            @pl.when(sends(t))
            def _():
                if t:
                    hop(chunk, c, t - 1, to_right).wait_recv()
                hop(chunk, c, t, to_right).start()

    def line_finish(chunk, c):
        for to_right, end in ((True, last), (False, 0)):

            @pl.when(g == end)
            def _():
                for t in range(last):
                    hop(chunk, c, t, to_right).wait_recv()

    mine = {}

    def swap_start(chunk):
        go(swap(chunk))
        mine[chunk] = pltpu.make_async_copy(mix.at[x, chunk], gat.at[chunk, g, x], mine_sem.at[chunk])
        mine[chunk].start()

    def line_sent(chunk):
        for c in range(2):
            for t in range(last):

                @pl.when(sends_right(t))
                def _():
                    hop(chunk, c, t, True).wait_send()

                @pl.when(sends_left(t))
                def _():
                    hop(chunk, c, t, False).wait_send()

    def hidden_left(chunk):
        for xs in range(2):
            for s in range(groups):
                start = (xs * groups + s) * width
                left[:, start : start + width] = gat[chunk, s, xs].reshape(hid.shape[0], width)

    def hidden_tile(n):
        rows, tile = hid.shape[0], HIDDEN_TILE
        columns = slice(n * tile, (n + 1) * tile)
        total = jnp.dot(
            left[...], wl[:, :, :, columns].reshape(left.shape[1], tile),
            preferred_element_type=jnp.float32,
        )
        value, tangent = gelu_pair(total[: rows // 2], total[rows // 2 :])
        hid[: rows // 2, columns] = value.astype(jnp.bfloat16)
        hid[rows // 2 :, columns] = tangent.astype(jnp.bfloat16)

    def out_slices(chunk, m):
        wide = 2 * span
        total = jnp.dot(
            hid[...], wol[:, :, :, m * wide : (m + 1) * wide].reshape(hid.shape[1], wide),
            preferred_element_type=jnp.float32,
        ).astype(jnp.bfloat16)
        for kind in range(2):
            for c in range(2):
                at = (kind * 2 + c) * half
                for n in range(2):
                    part[chunk, c, 2 * m + n, kind] = total[at : at + half, n * span : (n + 1) * span]

    def sum_copy(to_up, chunk, c, n):
        way = 0 if to_up else 1
        return remote(
            part.at[chunk, c, n], arrived.at[way, chunk, c, n],
            rs_send.at[way, chunk, c, n], rs_recv.at[way, chunk, c, n], up if to_up else down,
        )

    def add_in(to_up, chunk, c, n):
        sum_copy(to_up, chunk, c, n).wait_recv()
        way = 0 if to_up else 1
        part[chunk, c, n] = (
            part[chunk, c, n].astype(jnp.float32) + arrived[way, chunk, c, n].astype(jnp.float32)
        ).astype(jnp.bfloat16)

    def sum_start(chunk, n, distance):
        for c in range(2):
            home = homes[chunk][c]
            if home == distance:

                @pl.when(g == 0)
                def _():
                    sum_copy(True, chunk, c, n).start()

            if home == last - distance:

                @pl.when(g == last)
                def _():
                    sum_copy(False, chunk, c, n).start()

    def sum_step(chunk, n, distance):
        for c in range(2):
            home = homes[chunk][c]
            if distance < home:

                @pl.when(g == distance)
                def _():
                    add_in(True, chunk, c, n)
                    sum_copy(True, chunk, c, n).start()

            if last - distance > home:

                @pl.when(g == last - distance)
                def _():
                    add_in(False, chunk, c, n)
                    sum_copy(False, chunk, c, n).start()

    def out_copies(n, local):
        side, start = divmod(n * span, feats)
        made = []
        for kind, ref in enumerate((out_main, out_tangent)):
            dst = ref.at[pl.ds(pl.multiple_of(x * half, half), half), pl.ds(start, span)]
            if local:
                made.append(pltpu.make_async_copy(fin.at[n, kind], dst, out_sem.at[n, kind]))
            else:
                made.append(remote(fin.at[n, kind], dst, out_send.at[n, kind], out_recv.at[n, kind], twin))
        return side, made

    def sum_final(chunk, n):
        for c in range(2):
            home = homes[chunk][c]

            @pl.when(g == home)
            def _():
                total = part[chunk, c, n].astype(jnp.float32)
                for way, needed in ((0, home > 0), (1, home < last)):
                    if needed:
                        sum_copy(way == 0, chunk, c, n).wait_recv()
                        total = total + arrived[way, chunk, c, n].astype(jnp.float32)
                for kind in range(2):
                    at = (kind * 2 + c) * half
                    for m in range(span // width):
                        s = (n * span % feats) // width + m
                        fin[n, kind, :, m * width : (m + 1) * width] = (
                            gat[chunk, s, n * span // feats, kind, c].astype(jnp.float32)
                            + total[kind, :, m * width : (m + 1) * width]
                        ).astype(jnp.bfloat16)
                side, local = out_copies(n, True)
                _, far = out_copies(n, False)

                @pl.when(x == side)
                def _():
                    for copy in local:
                        copy.start()

                @pl.when(x != side)
                def _():
                    for copy in far:
                        copy.start()

    sends = (2, 0, 1)
    w_in_first_pieces = ((2, 0), (2, 1), (0, 0), (1, 0))
    w_in_last_pieces = ((0, 1), (1, 1))
    inner = (g > 0) & (g < last)
    outer = (g == 0) | (g == last)

    def w_in_send(pieces):
        for r, p in pieces:
            wz_start(r, p).start()

    for j in range(8):
        for r in sends:
            z_start(r, j)

    @pl.when(inner)
    def _():
        w_in_send(w_in_first_pieces)

    locals_ = [pltpu.make_async_copy(piece(j, g), slot(j, g), own_sem.at[j]) for j in range(8)]
    for copy in locals_:
        copy.start()
    w_locals = [
        pltpu.make_async_copy(w_in_piece(g, p), w_in_slot(x, i, (g, p)), w_sem.at[p])
        for p in range(cuts)
    ] + [pltpu.make_async_copy(w_out, wol.at[x, i], w_sem.at[cuts])]
    for copy in w_locals:
        copy.start()
    for j in range(4):
        locals_[j].wait()
        kv_spread(3, j)
    for p in range(cuts):
        gi_start((g, p), (3, p), w_in_piece(g, p))
    for r in range(parts - 1):
        go_start(r, r, w_out_piece(r), (1,))

    def take(*which):
        for r, j in which:
            z_wait(r, j)
            kv_spread(r, j)

    def onward(*which):
        for r, j in which:
            kv_forward(r, j)

    def w_out_start(r):
        go_start(r, r, w_out_piece(r), (0, 2))

    take((2, 0), (0, 0))
    w_out_start(0)
    take((2, 1), (0, 1), (1, 0))
    onward((3, 0), (3, 1), (3, 2), (3, 3))
    for p in range(cuts):
        w_in_first(3, p)
    take((2, 2), (0, 2), (2, 3), (0, 3))
    w_out_start(1)
    for p in range(cuts):
        w_in_rest(3, p)
    onward((2, 0), (0, 0), (2, 1), (0, 1), (1, 0))
    go_first(0, 0)
    take((1, 1))
    w_out_start(2)
    onward((2, 2), (0, 2), (2, 3), (0, 3))
    w_out_rest(0)
    take((1, 2))
    onward((1, 1))
    go_first(1, 1)
    take((1, 3))
    go_first(2, 2)
    w_out_rest(1)
    onward((1, 2), (1, 3))
    w_out_rest(2)
    for j in range(4, 8):
        locals_[j].wait()
        for r in (2, 0, 1):
            z_wait(r, j)
        if j == 6:


            @pl.when(outer)
            def _():
                w_in_send(w_in_first_pieces)

    for j in range(4):
        for r in range(groups):
            kv_finish(r, j)
    attend_head(0, 0)
    w_in_start(2, 0)
    attend_head(0, 1)
    attend_head(0, 2)
    swap_start(0)
    line_step(0, 0, 0)
    w_in_start(2, 1)
    w_in_first(2, 0)
    attend_head(1, 0)
    w_in_start(1, 0)
    line_step(0, 1, 0)
    w_in_send(w_in_last_pieces)
    w_in_rest(2, 0)
    w_in_first(2, 1)
    attend_head(1, 1)
    w_in_rest(2, 1)
    w_in_first(1, 0)
    attend_head(1, 2)
    w_in_start(0, 0)
    line_step(0, 0, 1)
    w_in_rest(1, 0)
    w_in_first(0, 0)
    line_step(0, 1, 1)
    w_in_rest(0, 0)
    w_in_start(1, 1)
    w_in_start(0, 1)
    line_step(0, 0, 2)
    line_step(0, 1, 2)
    line_step(1, 0, 0)
    w_in_first(1, 1)
    w_in_first(0, 1)
    swap_start(1)
    w_in_rest(1, 1)
    go_start(3, 3, w_out_piece(3))
    w_in_rest(0, 1)
    line_step(1, 1, 0)
    line_step(1, 0, 1)
    for copy in w_locals:
        copy.wait()
    for p in range(cuts):
        for r in range(groups):
            gi_finish((ranks[r], p), (r, p))
    line_finish(0, 0)
    line_finish(0, 1)
    mine[0].wait()
    hidden_left(0)
    tiles = hid.shape[1] // HIDDEN_TILE
    for n in range(tiles):
        hidden_tile(n)
        if n == 0:
            line_step(1, 1, 1)
            go_first(3, 3)
        else:
            line_step(1, 0, 2)
    for r in range(parts - 1):
        go_finish(r, r)
    pairs = slices // 2
    order = [m for both in zip(range(pairs // 2), range(pairs // 2, pairs)) for m in both]
    order_n = [2 * m + n for m in order for n in range(2)]
    waiting = list(order_n)

    def sum_next(count):
        for n in waiting[:count]:
            sum_step(0, n, 1)
        del waiting[:count]

    for m in order:
        if m == order[1]:
            line_step(1, 1, 2)
        if m == order[-1]:
            w_out_rest(3)
            go_finish(3, 3)
        out_slices(0, m)
        for n in range(2):
            sum_start(0, 2 * m + n, 2)
        if m == order[1] or m == order[2]:
            sum_next(2)
    for n in order_n[:2]:
        sum_start(0, n, 1)
    for c in range(2):
        line_finish(1, c)
    mine[1].wait()
    hidden_left(1)
    sum_next(1)
    for n in range(tiles):
        hidden_tile(n)
        sum_next(1)
    for m in order:
        out_slices(1, m)
        for n in range(2):
            sum_start(1, 2 * m + n, 3)
        sum_next(1)
    for n in order_n[2:]:
        sum_start(0, n, 1)
    for at in range(slices + 2):
        if at < slices:
            sum_step(1, order_n[at], 1)
        if 0 < at <= slices:
            sum_step(1, order_n[at - 1], 2)
        if at > 1:
            sum_final(1, order_n[at - 2])
    for n in order_n:
        sum_final(0, n)
    for n in range(slices):
        side, local = out_copies(n, True)
        _, far = out_copies(n, False)

        @pl.when(x == side)
        def _():
            for copy in local:
                copy.wait()
            for copy in far:
                copy.wait_recv()

        @pl.when(x != side)
        def _():
            for copy in far:
                copy.wait_send()

    for copy in sent:
        copy.wait_send()
    for p in range(cuts):
        for r in range(last):
            wz_start(r, p).wait_send()
    for chunk in range(2):
        line_sent(chunk)
        for c in range(2):
            home = homes[chunk][c]
            for n in range(slices):

                @pl.when(g < home)
                def _():
                    sum_copy(True, chunk, c, n).wait_send()

                @pl.when(g > home)
                def _():
                    sum_copy(False, chunk, c, n).wait_send()


SLICES = 8
PARTS = 4
CUTS = 2
HIDDEN_TILE = 896


def by_layers(query, key, value, d_query, d_key, d_value, residual, d_residual, w_in, w_out, dp, seq):
    groups = seq // INNER
    rows, feats = query.shape
    half, width = rows // dp, feats // groups
    deep, hidden = w_in.shape[0], w_in.shape[1] // groups
    whole = dp * feats
    span = whole // SLICES
    dma = pltpu.SemaphoreType.DMA
    low = jnp.bfloat16
    last = groups - 1
    length = groups * INNER * rows
    flops = 12 * groups * rows * length * width + 8 * dp * hidden * whole * groups * half * 2
    return tuple(pl.pallas_call(
        block_kernel,
        in_specs=[pl.BlockSpec(memory_space=pl.ANY)] * 10,
        out_specs=[pl.BlockSpec(memory_space=pl.ANY)] * 2,
        out_shape=[jax.ShapeDtypeStruct((rows, feats), low)] * 2,
        scratch_shapes=[
            pltpu.VMEM((4, groups, rows, width), low),
            pltpu.VMEM((INNER, groups, 4, rows, width), low),
            pltpu.VMEM((groups, INNER, deep, dp * hidden), low),
            pltpu.VMEM((dp, INNER, w_out.shape[0], whole), low),
            pltpu.VMEM((dp, 2, 2, 2, half, width), low),
            pltpu.VMEM((2, groups, dp, 2, 2, half, width), low),
            pltpu.VMEM((4 * half, whole), low),
            pltpu.VMEM((4 * half, dp * hidden), low),
            pltpu.VMEM((2, 2, SLICES, 2, half, span), low),
            pltpu.VMEM((2, 2, 2, SLICES, 2, half, span), low),
            pltpu.VMEM((SLICES, 2, half, span), low),
            dma((last, 8)), dma((groups, 8)), dma((8,)),
        ]
        + [dma((groups, 4)) for _ in range(6)]
        + [dma((last, CUTS)), dma((groups, CUTS)), dma((groups, CUTS, 7)), dma((groups, CUTS, 7))]
        + [dma((PARTS, 7)), dma((PARTS, 7)), dma((CUTS + 1,))]
        + [dma((2,)), dma((2,)), dma((2,))]
        + [dma((2, 2, last)) for _ in range(4)]
        + [dma((2, 2, 2, SLICES)), dma((2, 2, 2, SLICES))]
        + [dma((SLICES, 2)) for _ in range(3)],
        cost_estimate=pl.CostEstimate(flops=flops, bytes_accessed=10**8, transcendentals=0),
        compiler_params=pltpu.CompilerParams(
            collective_id=0, has_side_effects=True, vmem_limit_bytes=60 * 2**20
        ),
        name="block",
    )(query, d_query, residual, d_residual, key, value, d_key, d_value, w_in, w_out))


def on_device(*args, dp, seq):
    query, w_in = args[0], args[8]
    groups = seq // INNER
    tile = groups * HEAD_DIM
    if dp != 2 or seq % INNER or groups != 4 or query.shape[1] % tile or w_in.shape[1] % tile:
        return by_rows(*args)
    return by_layers(*args, dp=dp, seq=seq)


def solution(mesh):
    in_specs = (P("seq", "dp"),) * 9 + (P(("dp", "seq"), None),)
    out_specs = (P("seq", "dp"), P("seq", "dp"))
    body = functools.partial(on_device, dp=mesh.shape["dp"], seq=mesh.shape["seq"])
    return jax.shard_map(
        body, mesh=mesh, in_specs=in_specs, out_specs=out_specs, check_vma=False
    )
```

```python
import functools
import math

import jax
import jax.numpy as jnp
from jax import lax
from jax.experimental import pallas as pl
from jax.experimental.pallas import tpu as pltpu
from jax.sharding import PartitionSpec as P

HEAD_DIM = 128


gelu_coeff = 0.7978845608
cubic_coeff = 0.044715


def gelu_pair(pre_act, d_pre_act):
    inner_arg = gelu_coeff * (pre_act + cubic_coeff * pre_act * pre_act * pre_act)
    hyper = jnp.tanh(inner_arg)
    gelu_value = 0.5 * pre_act * (1.0 + hyper)
    gelu_slope = 0.5 * (1.0 + hyper) + 0.5 * pre_act * (1.0 - hyper * hyper) * gelu_coeff * (
        1.0 + 3.0 * cubic_coeff * pre_act * pre_act
    )
    return (gelu_value, gelu_slope * d_pre_act)


def nt(a, b):
    return lax.dot_general(a, b, (((1,), (1,)), ((), ())), preferred_element_type=jnp.float32)


def attend_math(q, dq, res, dres, keys, values, keys_pair, values_pair):
    scale = 1.0 / math.sqrt(HEAD_DIM)
    scores = nt(q, keys) * scale
    d_scores = nt(jnp.concatenate([dq, q], axis=1), keys_pair) * scale
    peak = jnp.max(scores, axis=1, keepdims=True)
    weights = jnp.exp(scores - peak)
    mixed = weights * d_scores
    total = jnp.sum(weights, axis=1, keepdims=True)
    slope = jnp.sum(mixed, axis=1, keepdims=True)
    both = jnp.dot(weights.astype(jnp.bfloat16), values_pair, preferred_element_type=jnp.float32)
    tangent = both[:, HEAD_DIM:] + jnp.dot(
        mixed.astype(jnp.bfloat16), values, preferred_element_type=jnp.float32
    )
    attended = both[:, :HEAD_DIM] / total
    d_attended = tangent / total - (slope / total) * attended
    return (
        (res.astype(jnp.float32) + attended).astype(jnp.bfloat16),
        (dres.astype(jnp.float32) + d_attended).astype(jnp.bfloat16),
    )


def attend_kernel(q, dq, res, dres, k, v, dk, dv, out, *, rows):
    keys, values = k[...], v[...]
    keys_pair = jnp.concatenate([keys, dk[...]], axis=1)
    values_pair = jnp.concatenate([values, dv[...]], axis=1)
    for start in range(0, q.shape[0], rows):
        part = pl.ds(start, rows)
        out[0, part, :], out[1, part, :] = attend_math(
            q[part, :], dq[part, :], res[part, :], dres[part, :],
            keys, values, keys_pair, values_pair,
        )


def attend(query, d_query, residual, d_residual, kv):
    rows, feats = query.shape
    heads = feats // HEAD_DIM
    length = kv.shape[0]
    own = pl.BlockSpec((rows, HEAD_DIM), lambda h: (0, h))

    def kv_spec(i):
        return pl.BlockSpec((length, HEAD_DIM), lambda h: (0, i * heads + h))

    return pl.pallas_call(
        functools.partial(attend_kernel, rows=min(rows, 128)),
        grid=(heads,),
        in_specs=[own] * 4 + [kv_spec(i) for i in range(4)],
        out_specs=pl.BlockSpec((2, rows, HEAD_DIM), lambda h: (0, 0, h)),
        out_shape=jax.ShapeDtypeStruct((2, rows, feats), jnp.bfloat16),
        cost_estimate=pl.CostEstimate(
            flops=12 * rows * length * feats, bytes_accessed=8 * length * feats, transcendentals=0
        ),
        name="attend",
    )(query, d_query, residual, d_residual, kv, kv, kv, kv)


def by_rows(query, key, value, d_query, d_key, d_value, residual, d_residual, w_in, w_out):
    rows, feats = query.shape
    kv = lax.all_gather(
        jnp.concatenate([key, value, d_key, d_value], axis=1), "seq", axis=0, tiled=True
    )
    w_in_whole = lax.all_gather(w_in, "seq", axis=0, tiled=True)
    w_out_whole = lax.all_gather(w_out, "seq", axis=0, tiled=True)
    mixed = attend(query, d_query, residual, d_residual, kv).reshape(2 * rows, feats)
    whole = lax.all_gather(mixed, "dp", axis=1, tiled=True)
    pre = jnp.dot(whole, w_in_whole, preferred_element_type=jnp.float32)
    hidden, d_hidden = gelu_pair(pre[:rows], pre[rows:])
    hidden = jnp.concatenate([hidden.astype(jnp.bfloat16), d_hidden.astype(jnp.bfloat16)], axis=0)
    partial = jnp.dot(hidden, w_out_whole, preferred_element_type=jnp.float32)
    summed = lax.psum_scatter(
        partial.astype(jnp.bfloat16), "dp", scatter_dimension=1, tiled=True
    ).astype(jnp.float32)
    out = (mixed.astype(jnp.float32) + summed).astype(jnp.bfloat16)
    return (out[:rows], out[rows:])


INNER = 4
MESH = pl.DeviceIdType.MESH
COMM_COST = pl.CostEstimate(flops=10**11, bytes_accessed=10**8, transcendentals=0)


def place(groups):
    seq = lax.axis_index("seq")
    return lax.axis_index("dp"), lax.div(seq, INNER), lax.rem(seq, INNER)


def enter(devices):
    barrier = pltpu.get_barrier_semaphore()
    for device in devices:
        pl.semaphore_signal(barrier, inc=1, device_id=device, device_id_type=MESH)
    pl.semaphore_wait(barrier, len(devices))


def block_kernel(
    q, dq, res, dres, k, v, dk, dv, w_in, w_out, out_main, out_tangent,
    own, kv, wl, wol, mix, gat, left, hid, part, arrived, fin,
    z_send, z_recv, own_sem, ky_send, ky_recv, kp_send, kp_recv, kf_send, kf_recv,
    wz_send, wz_recv, gi_send, gi_recv, go_send, go_recv, w_sem,
    swap_send, swap_recv, mine_sem, right_send, right_recv, left_send, left_recv,
    rs_send, rs_recv, out_send, out_recv, out_sem,
):
    groups, width = own.shape[1], own.shape[3]
    feats = q.shape[1]
    hidden = w_in.shape[1] // groups
    heads = width // HEAD_DIM
    half = mix.shape[4]
    last = groups - 1
    slices = fin.shape[0]
    span = fin.shape[3]
    parts = go_send.shape[0]
    wide_out = w_out.shape[1] // parts
    cuts = wz_send.shape[1]
    deep_in = w_in.shape[0] // cuts
    homes = ((1, 2), (0, 3))
    x, g, i = place(groups)
    other = 1 - x
    core = lax.rem(i, 2)
    next_i = i + 1 - 2 * core
    across_i = lax.rem(i + 2, INNER)
    partner = (x, g * INNER + next_i)
    across = (x, g * INNER + across_i)
    twin = (other, g * INNER + i)
    high = lax.div(g, 2)
    ranks = (last * (1 - high), 2 - high, g + 1 - 2 * lax.rem(g, 2), g)
    peers = [(x, to * INNER + i) for to in ranks[:last]]
    up = (x, jnp.minimum(g + 1, last) * INNER + i)
    down = (x, jnp.maximum(g - 1, 0) * INNER + i)
    enter(peers + [partner, across, twin])

    def remote(src, dst, send, recv, device):
        return pltpu.make_async_remote_copy(
            src_ref=src, dst_ref=dst, send_sem=send, recv_sem=recv,
            device_id=device, device_id_type=MESH,
        )

    sent = []

    def go(copy):
        copy.start()
        sent.append(copy)
        return copy

    def piece(j, to):
        ref = (k, v, dk, dv, q, dq, res, dres)[j]
        return ref.at[:, pl.ds(pl.multiple_of(to * width, 128), width)]

    def slot(j, source):
        return kv.at[i, source, j] if j < 4 else own.at[j - 4, source]

    def z_start(r, j):
        go(remote(piece(j, ranks[r]), slot(j, g), z_send.at[r, j], z_recv.at[g, j], peers[r]))

    def z_wait(r, j):
        source = ranks[r]
        remote(piece(j, source), slot(j, source), z_send.at[r, j], z_recv.at[source, j], peers[r]).wait_recv()

    def w_in_piece(to, p):
        return w_in.at[pl.ds(p * deep_in, deep_in), pl.ds(pl.multiple_of(to * hidden, 128), hidden)]

    def w_in_slot(xs, at, n):
        s, p = n
        columns = pl.ds(pl.multiple_of(xs * hidden, 128), hidden)
        return wl.at[s, at, pl.ds(p * deep_in, deep_in), columns]

    def w_out_piece(r):
        return w_out.at[:, pl.ds(r * wide_out, wide_out)]

    def w_out_slot(xs, at, r):
        return wol.at[xs, at, :, pl.ds(r * wide_out, wide_out)]

    def gather(slot_of, send, recv, first, second, first_at, second_at):
        def copy(which, src_at, n, idx, device, src=None):
            dst = slot_of(src_at[0], src_at[1], n)
            at = idx if isinstance(idx, tuple) else (idx,)
            return remote(src if src is not None else dst, dst,
                          send.at[at + (which,)], recv.at[at + (which,)], device)

        def start(n, idx, src=None, which=(0, 1, 2)):
            for to in which:
                go(copy(to, (x, i), n, idx, (first, second, partner)[to], src))

        def wait(which, at, n, idx):
            copy(which, at, n, idx, partner).wait_recv()

        def from_first(n, idx):
            wait(0, first_at, n, idx)
            go(copy(3, first_at, n, idx, second))
            go(copy(4, first_at, n, idx, partner))

        def from_second(n, idx):
            wait(1, second_at, n, idx)
            go(copy(5, second_at, n, idx, partner))

        def from_far(n, idx):
            far = (other, across_i)
            wait(3, far, n, idx)
            go(copy(6, far, n, idx, partner))

        def finish(n, idx):
            for which, at in ((2, (x, i)), (4, first_at), (5, second_at), (6, (other, across_i))):
                wait(which, (at[0], at[1] + 1 - 2 * lax.rem(at[1], 2)), n, idx)

        return start, from_first, from_second, from_far, finish

    def pick(a, b):
        return tuple(jnp.where(core == 0, m, n) for m, n in zip(a, b))

    go_start, go_first, go_second, go_far, go_finish = gather(
        w_out_slot, go_send, go_recv, across, twin, (x, across_i), (other, i),
    )
    gi_start, gi_first, gi_second, gi_far, gi_finish = gather(
        w_in_slot, gi_send, gi_recv, pick(twin, across), pick(across, twin),
        pick((other, i), (x, across_i)), pick((x, across_i), (other, i)),
    )

    def wz_start(r, p):
        return remote(
            w_in_piece(ranks[r], p), w_in_slot(x, i, (g, p)),
            wz_send.at[r, p], wz_recv.at[g, p], peers[r],
        )

    def w_in_first(t, p):
        gi_first((ranks[t], p), (t, p))

    def w_in_rest(t, p):
        gi_second((ranks[t], p), (t, p))
        gi_far((ranks[t], p), (t, p))

    def w_in_start(t, p):
        source = ranks[t]
        remote(
            w_in_piece(source, p), w_in_slot(x, i, (source, p)),
            wz_send.at[t, p], wz_recv.at[source, p], peers[t],
        ).wait_recv()
        gi_start((ranks[t], p), (t, p))

    def w_out_rest(r):
        go_second(r, r)
        go_far(r, r)

    def kv_copy(at, t, j, send, recv, device):
        block = kv.at[at, ranks[t], j]
        return remote(block, block, send.at[t, j], recv.at[t, j], device)

    def kv_spread(t, j):
        go(kv_copy(i, t, j, ky_send, ky_recv, across))
        go(kv_copy(i, t, j, kp_send, kp_recv, partner))

    def kv_forward(t, j):
        kv_copy(across_i, t, j, ky_send, ky_recv, across).wait_recv()
        go(kv_copy(across_i, t, j, kf_send, kf_recv, partner))

    def kv_finish(t, j):
        kv_copy(next_i, t, j, kp_send, kp_recv, partner).wait_recv()
        at = across_i + 1 - 2 * lax.rem(across_i, 2)
        kv_copy(at, t, j, kf_send, kf_recv, partner).wait_recv()

    def attend_head(chunk, h):
        feat = pl.ds(h * HEAD_DIM, HEAD_DIM)
        length = kv.shape[0] * kv.shape[1] * kv.shape[3]
        keys, values, d_keys, d_values = (
            kv[:, :, j, :, feat].reshape(length, HEAD_DIM) for j in range(4)
        )
        keys_pair = jnp.concatenate([keys, d_keys], axis=1)
        values_pair = jnp.concatenate([values, d_values], axis=1)
        for c in range(2):
            home = homes[chunk][c]
            pair = attend_math(
                own[0, home, :, feat], own[1, home, :, feat],
                own[2, home, :, feat], own[3, home, :, feat],
                keys, values, keys_pair, values_pair,
            )
            for side in range(2):
                for kind in range(2):
                    mix[side, chunk, kind, c, :, feat] = pair[kind][side * half : (side + 1) * half]

    def swap(chunk):
        return remote(mix.at[other, chunk], gat.at[chunk, g, x],
                      swap_send.at[chunk], swap_recv.at[chunk], twin)

    def hop(chunk, c, t, to_right):
        source = g - t if to_right else g + t
        sends, recvs = (right_send, right_recv) if to_right else (left_send, left_recv)
        side = other if c else x
        return remote(
            mix.at[x, chunk] if c == 0 and t == 0 else gat.at[chunk, source, side],
            gat.at[chunk, source, side],
            sends.at[chunk, c, t], recvs.at[chunk, c, t], up if to_right else down,
        )

    def sends_right(t):
        return (g >= t) & (g < last)

    def sends_left(t):
        return (g + t <= last) & (g > 0)

    def line_step(chunk, c, t):
        if t == 0 and c:
            swap(chunk).wait_recv()
        for to_right, sends in ((True, sends_right), (False, sends_left)):

            @pl.when(sends(t))
            def _():
                if t:
                    hop(chunk, c, t - 1, to_right).wait_recv()
                hop(chunk, c, t, to_right).start()

    def line_finish(chunk, c):
        for to_right, end in ((True, last), (False, 0)):

            @pl.when(g == end)
            def _():
                for t in range(last):
                    hop(chunk, c, t, to_right).wait_recv()

    mine = {}

    def swap_start(chunk):
        go(swap(chunk))
        mine[chunk] = pltpu.make_async_copy(mix.at[x, chunk], gat.at[chunk, g, x], mine_sem.at[chunk])
        mine[chunk].start()

    def line_sent(chunk):
        for c in range(2):
            for t in range(last):

                @pl.when(sends_right(t))
                def _():
                    hop(chunk, c, t, True).wait_send()

                @pl.when(sends_left(t))
                def _():
                    hop(chunk, c, t, False).wait_send()

    def hidden_left(chunk):
        for xs in range(2):
            for s in range(groups):
                start = (xs * groups + s) * width
                left[:, start : start + width] = gat[chunk, s, xs].reshape(hid.shape[0], width)

    def hidden_tile(n):
        rows, tile = hid.shape[0], HIDDEN_TILE
        columns = slice(n * tile, (n + 1) * tile)
        total = jnp.dot(
            left[...], wl[:, :, :, columns].reshape(left.shape[1], tile),
            preferred_element_type=jnp.float32,
        )
        value, tangent = gelu_pair(total[: rows // 2], total[rows // 2 :])
        hid[: rows // 2, columns] = value.astype(jnp.bfloat16)
        hid[rows // 2 :, columns] = tangent.astype(jnp.bfloat16)

    def out_slices(chunk, m):
        wide = 2 * span
        total = jnp.dot(
            hid[...], wol[:, :, :, m * wide : (m + 1) * wide].reshape(hid.shape[1], wide),
            preferred_element_type=jnp.float32,
        ).astype(jnp.bfloat16)
        for kind in range(2):
            for c in range(2):
                at = (kind * 2 + c) * half
                for n in range(2):
                    part[chunk, c, 2 * m + n, kind] = total[at : at + half, n * span : (n + 1) * span]

    def sum_copy(to_up, chunk, c, n):
        way = 0 if to_up else 1
        return remote(
            part.at[chunk, c, n], arrived.at[way, chunk, c, n],
            rs_send.at[way, chunk, c, n], rs_recv.at[way, chunk, c, n], up if to_up else down,
        )

    def add_in(to_up, chunk, c, n):
        sum_copy(to_up, chunk, c, n).wait_recv()
        way = 0 if to_up else 1
        part[chunk, c, n] = (
            part[chunk, c, n].astype(jnp.float32) + arrived[way, chunk, c, n].astype(jnp.float32)
        ).astype(jnp.bfloat16)

    def sum_start(chunk, n, distance):
        for c in range(2):
            home = homes[chunk][c]
            if home == distance:

                @pl.when(g == 0)
                def _():
                    sum_copy(True, chunk, c, n).start()

            if home == last - distance:

                @pl.when(g == last)
                def _():
                    sum_copy(False, chunk, c, n).start()

    def sum_step(chunk, n, distance):
        for c in range(2):
            home = homes[chunk][c]
            if distance < home:

                @pl.when(g == distance)
                def _():
                    add_in(True, chunk, c, n)
                    sum_copy(True, chunk, c, n).start()

            if last - distance > home:

                @pl.when(g == last - distance)
                def _():
                    add_in(False, chunk, c, n)
                    sum_copy(False, chunk, c, n).start()

    def out_copies(n, local):
        side, start = divmod(n * span, feats)
        made = []
        for kind, ref in enumerate((out_main, out_tangent)):
            dst = ref.at[pl.ds(pl.multiple_of(x * half, half), half), pl.ds(start, span)]
            if local:
                made.append(pltpu.make_async_copy(fin.at[n, kind], dst, out_sem.at[n, kind]))
            else:
                made.append(remote(fin.at[n, kind], dst, out_send.at[n, kind], out_recv.at[n, kind], twin))
        return side, made

    def sum_final(chunk, n):
        for c in range(2):
            home = homes[chunk][c]

            @pl.when(g == home)
            def _():
                total = part[chunk, c, n].astype(jnp.float32)
                for way, needed in ((0, home > 0), (1, home < last)):
                    if needed:
                        sum_copy(way == 0, chunk, c, n).wait_recv()
                        total = total + arrived[way, chunk, c, n].astype(jnp.float32)
                for kind in range(2):
                    at = (kind * 2 + c) * half
                    for m in range(span // width):
                        s = (n * span % feats) // width + m
                        fin[n, kind, :, m * width : (m + 1) * width] = (
                            gat[chunk, s, n * span // feats, kind, c].astype(jnp.float32)
                            + total[kind, :, m * width : (m + 1) * width]
                        ).astype(jnp.bfloat16)
                side, local = out_copies(n, True)
                _, far = out_copies(n, False)

                @pl.when(x == side)
                def _():
                    for copy in local:
                        copy.start()

                @pl.when(x != side)
                def _():
                    for copy in far:
                        copy.start()

    sends = (2, 0, 1)
    w_in_first_pieces = ((2, 0), (2, 1), (0, 0), (1, 0))
    w_in_last_pieces = ((0, 1), (1, 1))
    inner = (g > 0) & (g < last)
    outer = (g == 0) | (g == last)

    def w_in_send(pieces):
        for r, p in pieces:
            wz_start(r, p).start()

    for j in range(8):
        for r in sends:
            z_start(r, j)

    @pl.when(inner)
    def _():
        w_in_send(w_in_first_pieces)

    locals_ = [pltpu.make_async_copy(piece(j, g), slot(j, g), own_sem.at[j]) for j in range(8)]
    for copy in locals_:
        copy.start()
    w_locals = [
        pltpu.make_async_copy(w_in_piece(g, p), w_in_slot(x, i, (g, p)), w_sem.at[p])
        for p in range(cuts)
    ] + [pltpu.make_async_copy(w_out, wol.at[x, i], w_sem.at[cuts])]
    for copy in w_locals:
        copy.start()
    for j in range(4):
        locals_[j].wait()
        kv_spread(3, j)
    for p in range(cuts):
        gi_start((g, p), (3, p), w_in_piece(g, p))
    for r in range(parts - 1):
        go_start(r, r, w_out_piece(r), (1,))

    def take(*which):
        for r, j in which:
            z_wait(r, j)
            kv_spread(r, j)

    def onward(*which):
        for r, j in which:
            kv_forward(r, j)

    def w_out_start(r):
        go_start(r, r, w_out_piece(r), (0, 2))

    take((2, 0), (0, 0))
    w_out_start(0)
    take((2, 1), (0, 1), (1, 0))
    onward((3, 0), (3, 1), (3, 2), (3, 3))
    for p in range(cuts):
        w_in_first(3, p)
    take((2, 2), (0, 2), (2, 3), (0, 3))
    w_out_start(1)
    for p in range(cuts):
        w_in_rest(3, p)
    onward((2, 0), (0, 0), (2, 1), (0, 1), (1, 0))
    go_first(0, 0)
    take((1, 1))
    w_out_start(2)
    onward((2, 2), (0, 2), (2, 3), (0, 3))
    w_out_rest(0)
    take((1, 2))
    onward((1, 1))
    go_first(1, 1)
    take((1, 3))
    go_first(2, 2)
    w_out_rest(1)
    onward((1, 2), (1, 3))
    w_out_rest(2)
    for j in range(4, 8):
        locals_[j].wait()
        for r in (2, 0, 1):
            z_wait(r, j)
        if j == 6:


            @pl.when(outer)
            def _():
                w_in_send(w_in_first_pieces)

    for j in range(4):
        for r in range(groups):
            kv_finish(r, j)
    attend_head(0, 0)
    w_in_start(2, 0)
    attend_head(0, 1)
    attend_head(0, 2)
    swap_start(0)
    line_step(0, 0, 0)
    w_in_start(2, 1)
    w_in_first(2, 0)
    attend_head(1, 0)
    w_in_start(1, 0)
    line_step(0, 1, 0)
    w_in_send(w_in_last_pieces)
    w_in_rest(2, 0)
    w_in_first(2, 1)
    attend_head(1, 1)
    w_in_rest(2, 1)
    w_in_first(1, 0)
    attend_head(1, 2)
    w_in_start(0, 0)
    line_step(0, 0, 1)
    w_in_rest(1, 0)
    w_in_first(0, 0)
    line_step(0, 1, 1)
    w_in_rest(0, 0)
    w_in_start(1, 1)
    w_in_start(0, 1)
    line_step(0, 0, 2)
    line_step(0, 1, 2)
    line_step(1, 0, 0)
    w_in_first(1, 1)
    w_in_first(0, 1)
    swap_start(1)
    w_in_rest(1, 1)
    go_start(3, 3, w_out_piece(3))
    w_in_rest(0, 1)
    line_step(1, 1, 0)
    line_step(1, 0, 1)
    for copy in w_locals:
        copy.wait()
    for p in range(cuts):
        for r in range(groups):
            gi_finish((ranks[r], p), (r, p))
    line_finish(0, 0)
    line_finish(0, 1)
    mine[0].wait()
    hidden_left(0)
    tiles = hid.shape[1] // HIDDEN_TILE
    for n in range(tiles):
        hidden_tile(n)
        if n == 0:
            line_step(1, 1, 1)
            go_first(3, 3)
        else:
            line_step(1, 0, 2)
    for r in range(parts - 1):
        go_finish(r, r)
    pairs = slices // 2
    order = [m for both in zip(range(pairs // 2), range(pairs // 2, pairs)) for m in both]
    order_n = [2 * m + n for m in order for n in range(2)]
    waiting = list(order_n)

    def sum_next(count):
        for n in waiting[:count]:
            sum_step(0, n, 1)
        del waiting[:count]

    for m in order:
        if m == order[1]:
            line_step(1, 1, 2)
        if m == order[-1]:
            w_out_rest(3)
            go_finish(3, 3)
        out_slices(0, m)
        for n in range(2):
            sum_start(0, 2 * m + n, 2)
        if m == order[1] or m == order[2]:
            sum_next(2)
    for n in order_n[:2]:
        sum_start(0, n, 1)
    for c in range(2):
        line_finish(1, c)
    mine[1].wait()
    hidden_left(1)
    sum_next(1)
    for n in range(tiles):
        hidden_tile(n)
        sum_next(1)
    for m in order:
        out_slices(1, m)
        for n in range(2):
            sum_start(1, 2 * m + n, 3)
        sum_next(1)
    for n in order_n[2:]:
        sum_start(0, n, 1)
    for at in range(slices + 2):
        if at < slices:
            sum_step(1, order_n[at], 1)
        if 0 < at <= slices:
            sum_step(1, order_n[at - 1], 2)
        if at > 1:
            sum_final(1, order_n[at - 2])
    for n in order_n:
        sum_final(0, n)
    for n in range(slices):
        side, local = out_copies(n, True)
        _, far = out_copies(n, False)

        @pl.when(x == side)
        def _():
            for copy in local:
                copy.wait()
            for copy in far:
                copy.wait_recv()

        @pl.when(x != side)
        def _():
            for copy in far:
                copy.wait_send()

    for copy in sent:
        copy.wait_send()
    for p in range(cuts):
        for r in range(last):
            wz_start(r, p).wait_send()
    for chunk in range(2):
        line_sent(chunk)
        for c in range(2):
            home = homes[chunk][c]
            for n in range(slices):

                @pl.when(g < home)
                def _():
                    sum_copy(True, chunk, c, n).wait_send()

                @pl.when(g > home)
                def _():
                    sum_copy(False, chunk, c, n).wait_send()


def deliver_kernel(main, tangent, out_main, out_tangent):
    out_main[...] = main[...]
    out_tangent[...] = tangent[...]


def deliver(main, tangent):
    return pl.pallas_call(
        deliver_kernel,
        in_specs=[pl.BlockSpec(memory_space=pltpu.VMEM)] * 2,
        out_specs=[pl.BlockSpec(memory_space=pltpu.VMEM)] * 2,
        out_shape=[jax.ShapeDtypeStruct(main.shape, main.dtype)] * 2,
        name="deliver",
    )(main, tangent)


SLICES = 8
PARTS = 4
CUTS = 2
HIDDEN_TILE = 896


def by_layers(query, key, value, d_query, d_key, d_value, residual, d_residual, w_in, w_out, dp, seq):
    groups = seq // INNER
    rows, feats = query.shape
    half, width = rows // dp, feats // groups
    deep, hidden = w_in.shape[0], w_in.shape[1] // groups
    whole = dp * feats
    span = whole // SLICES
    dma = pltpu.SemaphoreType.DMA
    low = jnp.bfloat16
    last = groups - 1
    length = groups * INNER * rows
    flops = 12 * groups * rows * length * width + 8 * dp * hidden * whole * groups * half * 2
    return tuple(deliver(*pl.pallas_call(
        block_kernel,
        in_specs=[pl.BlockSpec(memory_space=pl.ANY)] * 10,
        out_specs=[pl.BlockSpec(memory_space=pl.ANY)] * 2,
        out_shape=[jax.ShapeDtypeStruct((rows, feats), low)] * 2,
        scratch_shapes=[
            pltpu.VMEM((4, groups, rows, width), low),
            pltpu.VMEM((INNER, groups, 4, rows, width), low),
            pltpu.VMEM((groups, INNER, deep, dp * hidden), low),
            pltpu.VMEM((dp, INNER, w_out.shape[0], whole), low),
            pltpu.VMEM((dp, 2, 2, 2, half, width), low),
            pltpu.VMEM((2, groups, dp, 2, 2, half, width), low),
            pltpu.VMEM((4 * half, whole), low),
            pltpu.VMEM((4 * half, dp * hidden), low),
            pltpu.VMEM((2, 2, SLICES, 2, half, span), low),
            pltpu.VMEM((2, 2, 2, SLICES, 2, half, span), low),
            pltpu.VMEM((SLICES, 2, half, span), low),
            dma((last, 8)), dma((groups, 8)), dma((8,)),
        ]
        + [dma((groups, 4)) for _ in range(6)]
        + [dma((last, CUTS)), dma((groups, CUTS)), dma((groups, CUTS, 7)), dma((groups, CUTS, 7))]
        + [dma((PARTS, 7)), dma((PARTS, 7)), dma((CUTS + 1,))]
        + [dma((2,)), dma((2,)), dma((2,))]
        + [dma((2, 2, last)) for _ in range(4)]
        + [dma((2, 2, 2, SLICES)), dma((2, 2, 2, SLICES))]
        + [dma((SLICES, 2)) for _ in range(3)],
        cost_estimate=pl.CostEstimate(flops=flops, bytes_accessed=10**8, transcendentals=0),
        compiler_params=pltpu.CompilerParams(
            collective_id=0, has_side_effects=True, vmem_limit_bytes=60 * 2**20
        ),
        name="block",
    )(query, d_query, residual, d_residual, key, value, d_key, d_value, w_in, w_out)))


def on_device(*args, dp, seq):
    query, w_in = args[0], args[8]
    groups = seq // INNER
    tile = groups * HEAD_DIM
    if dp != 2 or seq % INNER or groups != 4 or query.shape[1] % tile or w_in.shape[1] % tile:
        return by_rows(*args)
    return by_layers(*args, dp=dp, seq=seq)


def solution(mesh):
    in_specs = (P("seq", "dp"),) * 9 + (P(("dp", "seq"), None),)
    out_specs = (P("seq", "dp"), P("seq", "dp"))
    body = functools.partial(on_device, dp=mesh.shape["dp"], seq=mesh.shape["seq"])
    return jax.shard_map(
        body, mesh=mesh, in_specs=in_specs, out_specs=out_specs, check_vma=False
    )
```

```python
import functools
import math

import jax
import jax.numpy as jnp
from jax import lax
from jax.experimental import pallas as pl
from jax.experimental.pallas import tpu as pltpu
from jax.sharding import PartitionSpec as P

HEAD_DIM = 128


gelu_coeff = 0.7978845608
cubic_coeff = 0.044715


def gelu_pair(pre_act, d_pre_act):
    inner_arg = gelu_coeff * (pre_act + cubic_coeff * pre_act * pre_act * pre_act)
    hyper = jnp.tanh(inner_arg)
    gelu_value = 0.5 * pre_act * (1.0 + hyper)
    gelu_slope = 0.5 * (1.0 + hyper) + 0.5 * pre_act * (1.0 - hyper * hyper) * gelu_coeff * (
        1.0 + 3.0 * cubic_coeff * pre_act * pre_act
    )
    return (gelu_value, gelu_slope * d_pre_act)


def nt(a, b):
    return lax.dot_general(a, b, (((1,), (1,)), ((), ())), preferred_element_type=jnp.float32)


def attend_math(q, dq, res, dres, keys, values, keys_pair, values_pair):
    scale = 1.0 / math.sqrt(HEAD_DIM)
    scores = nt(q, keys) * scale
    d_scores = nt(jnp.concatenate([dq, q], axis=1), keys_pair) * scale
    peak = jnp.max(scores, axis=1, keepdims=True)
    weights = jnp.exp(scores - peak)
    mixed = weights * d_scores
    total = jnp.sum(weights, axis=1, keepdims=True)
    slope = jnp.sum(mixed, axis=1, keepdims=True)
    both = jnp.dot(weights.astype(jnp.bfloat16), values_pair, preferred_element_type=jnp.float32)
    tangent = both[:, HEAD_DIM:] + jnp.dot(
        mixed.astype(jnp.bfloat16), values, preferred_element_type=jnp.float32
    )
    attended = both[:, :HEAD_DIM] / total
    d_attended = tangent / total - (slope / total) * attended
    return (
        (res.astype(jnp.float32) + attended).astype(jnp.bfloat16),
        (dres.astype(jnp.float32) + d_attended).astype(jnp.bfloat16),
    )


def attend_kernel(q, dq, res, dres, k, v, dk, dv, out, *, rows):
    keys, values = k[...], v[...]
    keys_pair = jnp.concatenate([keys, dk[...]], axis=1)
    values_pair = jnp.concatenate([values, dv[...]], axis=1)
    for start in range(0, q.shape[0], rows):
        part = pl.ds(start, rows)
        out[0, part, :], out[1, part, :] = attend_math(
            q[part, :], dq[part, :], res[part, :], dres[part, :],
            keys, values, keys_pair, values_pair,
        )


def attend(query, d_query, residual, d_residual, kv):
    rows, feats = query.shape
    heads = feats // HEAD_DIM
    length = kv.shape[0]
    own = pl.BlockSpec((rows, HEAD_DIM), lambda h: (0, h))

    def kv_spec(i):
        return pl.BlockSpec((length, HEAD_DIM), lambda h: (0, i * heads + h))

    return pl.pallas_call(
        functools.partial(attend_kernel, rows=min(rows, 128)),
        grid=(heads,),
        in_specs=[own] * 4 + [kv_spec(i) for i in range(4)],
        out_specs=pl.BlockSpec((2, rows, HEAD_DIM), lambda h: (0, 0, h)),
        out_shape=jax.ShapeDtypeStruct((2, rows, feats), jnp.bfloat16),
        cost_estimate=pl.CostEstimate(
            flops=12 * rows * length * feats, bytes_accessed=8 * length * feats, transcendentals=0
        ),
        name="attend",
    )(query, d_query, residual, d_residual, kv, kv, kv, kv)


def by_rows(query, key, value, d_query, d_key, d_value, residual, d_residual, w_in, w_out):
    rows, feats = query.shape
    kv = lax.all_gather(
        jnp.concatenate([key, value, d_key, d_value], axis=1), "seq", axis=0, tiled=True
    )
    w_in_whole = lax.all_gather(w_in, "seq", axis=0, tiled=True)
    w_out_whole = lax.all_gather(w_out, "seq", axis=0, tiled=True)
    mixed = attend(query, d_query, residual, d_residual, kv).reshape(2 * rows, feats)
    whole = lax.all_gather(mixed, "dp", axis=1, tiled=True)
    pre = jnp.dot(whole, w_in_whole, preferred_element_type=jnp.float32)
    hidden, d_hidden = gelu_pair(pre[:rows], pre[rows:])
    hidden = jnp.concatenate([hidden.astype(jnp.bfloat16), d_hidden.astype(jnp.bfloat16)], axis=0)
    partial = jnp.dot(hidden, w_out_whole, preferred_element_type=jnp.float32)
    summed = lax.psum_scatter(
        partial.astype(jnp.bfloat16), "dp", scatter_dimension=1, tiled=True
    ).astype(jnp.float32)
    out = (mixed.astype(jnp.float32) + summed).astype(jnp.bfloat16)
    return (out[:rows], out[rows:])


INNER = 4
MESH = pl.DeviceIdType.MESH
COMM_COST = pl.CostEstimate(flops=10**11, bytes_accessed=10**8, transcendentals=0)


def place(groups):
    seq = lax.axis_index("seq")
    return lax.axis_index("dp"), lax.div(seq, INNER), lax.rem(seq, INNER)


def enter(devices):
    barrier = pltpu.get_barrier_semaphore()
    for device in devices:
        pl.semaphore_signal(barrier, inc=1, device_id=device, device_id_type=MESH)
    pl.semaphore_wait(barrier, len(devices))


def block_kernel(
    q, dq, res, dres, k, v, dk, dv, w_in, w_out, out_main, out_tangent,
    own, kv, wl, wol, mix, gat, hid, part, arrived, fin,
    z_send, z_recv, own_sem, ky_send, ky_recv, kp_send, kp_recv, kf_send, kf_recv,
    wz_send, wz_recv, gi_send, gi_recv, go_send, go_recv, w_sem,
    swap_send, swap_recv, mine_sem, right_send, right_recv, left_send, left_recv,
    rs_send, rs_recv, out_send, out_recv, out_sem,
):
    groups, width = own.shape[1], own.shape[3]
    feats = q.shape[1]
    hidden = w_in.shape[1] // groups
    heads = width // HEAD_DIM
    half = mix.shape[4]
    last = groups - 1
    slices = fin.shape[0]
    span = fin.shape[3]
    parts = go_send.shape[0]
    wide_out = w_out.shape[1] // parts
    cuts = wz_send.shape[1]
    deep_in = w_in.shape[0] // cuts
    homes = ((1, 2), (0, 3))
    x, g, i = place(groups)
    other = 1 - x
    core = lax.rem(i, 2)
    next_i = i + 1 - 2 * core
    across_i = lax.rem(i + 2, INNER)
    partner = (x, g * INNER + next_i)
    across = (x, g * INNER + across_i)
    twin = (other, g * INNER + i)
    high = lax.div(g, 2)
    ranks = (last * (1 - high), 2 - high, g + 1 - 2 * lax.rem(g, 2), g)
    peers = [(x, to * INNER + i) for to in ranks[:last]]
    up = (x, jnp.minimum(g + 1, last) * INNER + i)
    down = (x, jnp.maximum(g - 1, 0) * INNER + i)
    enter(peers + [partner, across, twin])

    def remote(src, dst, send, recv, device):
        return pltpu.make_async_remote_copy(
            src_ref=src, dst_ref=dst, send_sem=send, recv_sem=recv,
            device_id=device, device_id_type=MESH,
        )

    sent = []

    def go(copy):
        copy.start()
        sent.append(copy)
        return copy

    def piece(j, to):
        ref = (k, v, dk, dv, q, dq, res, dres)[j]
        return ref.at[:, pl.ds(pl.multiple_of(to * width, 128), width)]

    def slot(j, source):
        return kv.at[i, source, j] if j < 4 else own.at[j - 4, source]

    def z_start(r, j):
        go(remote(piece(j, ranks[r]), slot(j, g), z_send.at[r, j], z_recv.at[g, j], peers[r]))

    def z_wait(r, j):
        source = ranks[r]
        remote(piece(j, source), slot(j, source), z_send.at[r, j], z_recv.at[source, j], peers[r]).wait_recv()

    def w_in_piece(to, p):
        return w_in.at[pl.ds(p * deep_in, deep_in), pl.ds(pl.multiple_of(to * hidden, 128), hidden)]

    def w_in_slot(xs, at, n):
        s, p = n
        columns = pl.ds(pl.multiple_of(xs * hidden, 128), hidden)
        return wl.at[s, at, pl.ds(p * deep_in, deep_in), columns]

    def w_out_piece(r):
        return w_out.at[:, pl.ds(r * wide_out, wide_out)]

    def w_out_slot(xs, at, r):
        return wol.at[xs, at, :, pl.ds(r * wide_out, wide_out)]

    def gather(slot_of, send, recv, first, second, first_at, second_at):
        def copy(which, src_at, n, idx, device, src=None):
            dst = slot_of(src_at[0], src_at[1], n)
            at = idx if isinstance(idx, tuple) else (idx,)
            return remote(src if src is not None else dst, dst,
                          send.at[at + (which,)], recv.at[at + (which,)], device)

        def start(n, idx, src=None, which=(0, 1, 2)):
            for to in which:
                go(copy(to, (x, i), n, idx, (first, second, partner)[to], src))

        def wait(which, at, n, idx):
            copy(which, at, n, idx, partner).wait_recv()

        def from_first(n, idx):
            wait(0, first_at, n, idx)
            go(copy(3, first_at, n, idx, second))
            go(copy(4, first_at, n, idx, partner))

        def from_second(n, idx):
            wait(1, second_at, n, idx)
            go(copy(5, second_at, n, idx, partner))

        def from_far(n, idx):
            far = (other, across_i)
            wait(3, far, n, idx)
            go(copy(6, far, n, idx, partner))

        def finish(n, idx):
            for which, at in ((2, (x, i)), (4, first_at), (5, second_at), (6, (other, across_i))):
                wait(which, (at[0], at[1] + 1 - 2 * lax.rem(at[1], 2)), n, idx)

        return start, from_first, from_second, from_far, finish

    def pick(a, b):
        return tuple(jnp.where(core == 0, m, n) for m, n in zip(a, b))

    go_start, go_first, go_second, go_far, go_finish = gather(
        w_out_slot, go_send, go_recv, across, twin, (x, across_i), (other, i),
    )
    gi_start, gi_first, gi_second, gi_far, gi_finish = gather(
        w_in_slot, gi_send, gi_recv, pick(twin, across), pick(across, twin),
        pick((other, i), (x, across_i)), pick((x, across_i), (other, i)),
    )

    def wz_start(r, p):
        return remote(
            w_in_piece(ranks[r], p), w_in_slot(x, i, (g, p)),
            wz_send.at[r, p], wz_recv.at[g, p], peers[r],
        )

    def w_in_first(t, p):
        gi_first((ranks[t], p), (t, p))

    def w_in_rest(t, p):
        gi_second((ranks[t], p), (t, p))
        gi_far((ranks[t], p), (t, p))

    def w_in_start(t, p):
        source = ranks[t]
        remote(
            w_in_piece(source, p), w_in_slot(x, i, (source, p)),
            wz_send.at[t, p], wz_recv.at[source, p], peers[t],
        ).wait_recv()
        gi_start((ranks[t], p), (t, p))

    def w_out_rest(r):
        go_second(r, r)
        go_far(r, r)

    def kv_copy(at, t, j, send, recv, device):
        block = kv.at[at, ranks[t], j]
        return remote(block, block, send.at[t, j], recv.at[t, j], device)

    def kv_spread(t, j):
        go(kv_copy(i, t, j, ky_send, ky_recv, across))
        go(kv_copy(i, t, j, kp_send, kp_recv, partner))

    def kv_forward(t, j):
        kv_copy(across_i, t, j, ky_send, ky_recv, across).wait_recv()
        go(kv_copy(across_i, t, j, kf_send, kf_recv, partner))

    def kv_finish(t, j):
        kv_copy(next_i, t, j, kp_send, kp_recv, partner).wait_recv()
        at = across_i + 1 - 2 * lax.rem(across_i, 2)
        kv_copy(at, t, j, kf_send, kf_recv, partner).wait_recv()

    def attend_head(chunk, h):
        feat = pl.ds(h * HEAD_DIM, HEAD_DIM)
        length = kv.shape[0] * kv.shape[1] * kv.shape[3]
        keys, values, d_keys, d_values = (
            kv[:, :, j, :, feat].reshape(length, HEAD_DIM) for j in range(4)
        )
        keys_pair = jnp.concatenate([keys, d_keys], axis=1)
        values_pair = jnp.concatenate([values, d_values], axis=1)
        for c in range(2):
            home = homes[chunk][c]
            pair = attend_math(
                own[0, home, :, feat], own[1, home, :, feat],
                own[2, home, :, feat], own[3, home, :, feat],
                keys, values, keys_pair, values_pair,
            )
            for side in range(2):
                for kind in range(2):
                    mix[side, chunk, kind, c, :, feat] = pair[kind][side * half : (side + 1) * half]

    def swap(chunk):
        return remote(mix.at[other, chunk], gat.at[chunk, g, x],
                      swap_send.at[chunk], swap_recv.at[chunk], twin)

    def hop(chunk, c, t, to_right):
        source = g - t if to_right else g + t
        sends, recvs = (right_send, right_recv) if to_right else (left_send, left_recv)
        side = other if c else x
        return remote(
            mix.at[x, chunk] if c == 0 and t == 0 else gat.at[chunk, source, side],
            gat.at[chunk, source, side],
            sends.at[chunk, c, t], recvs.at[chunk, c, t], up if to_right else down,
        )

    def sends_right(t):
        return (g >= t) & (g < last)

    def sends_left(t):
        return (g + t <= last) & (g > 0)

    def line_step(chunk, c, t):
        if t == 0 and c:
            swap(chunk).wait_recv()
        for to_right, sends in ((True, sends_right), (False, sends_left)):

            @pl.when(sends(t))
            def _():
                if t:
                    hop(chunk, c, t - 1, to_right).wait_recv()
                hop(chunk, c, t, to_right).start()

    def line_finish(chunk, c):
        for to_right, end in ((True, last), (False, 0)):

            @pl.when(g == end)
            def _():
                for t in range(last):
                    hop(chunk, c, t, to_right).wait_recv()

    mine = {}

    def swap_start(chunk):
        go(swap(chunk))
        mine[chunk] = pltpu.make_async_copy(mix.at[x, chunk], gat.at[chunk, g, x], mine_sem.at[chunk])
        mine[chunk].start()

    def line_sent(chunk):
        for c in range(2):
            for t in range(last):

                @pl.when(sends_right(t))
                def _():
                    hop(chunk, c, t, True).wait_send()

                @pl.when(sends_left(t))
                def _():
                    hop(chunk, c, t, False).wait_send()

    def hidden_left(chunk):
        return jnp.concatenate(
            [gat[chunk, s, xs].reshape(hid.shape[0], width) for xs in range(2) for s in range(groups)],
            axis=1,
        )

    def hidden_tile(left, n):
        rows, tile = hid.shape[0], HIDDEN_TILE
        columns = slice(n * tile, (n + 1) * tile)
        total = jnp.dot(
            left, wl[:, :, :, columns].reshape(left.shape[1], tile),
            preferred_element_type=jnp.float32,
        )
        value, tangent = gelu_pair(total[: rows // 2], total[rows // 2 :])
        hid[: rows // 2, columns] = value.astype(jnp.bfloat16)
        hid[rows // 2 :, columns] = tangent.astype(jnp.bfloat16)

    def out_slices(chunk, m):
        wide = 2 * span
        total = jnp.dot(
            hid[...], wol[:, :, :, m * wide : (m + 1) * wide].reshape(hid.shape[1], wide),
            preferred_element_type=jnp.float32,
        ).astype(jnp.bfloat16)
        for kind in range(2):
            for c in range(2):
                at = (kind * 2 + c) * half
                for n in range(2):
                    part[chunk, c, 2 * m + n, kind] = total[at : at + half, n * span : (n + 1) * span]

    def sum_copy(to_up, chunk, c, n):
        way = 0 if to_up else 1
        return remote(
            part.at[chunk, c, n], arrived.at[way, chunk, c, n],
            rs_send.at[way, chunk, c, n], rs_recv.at[way, chunk, c, n], up if to_up else down,
        )

    def add_in(to_up, chunk, c, n):
        sum_copy(to_up, chunk, c, n).wait_recv()
        way = 0 if to_up else 1
        part[chunk, c, n] = (
            part[chunk, c, n].astype(jnp.float32) + arrived[way, chunk, c, n].astype(jnp.float32)
        ).astype(jnp.bfloat16)

    def sum_start(chunk, n, distance):
        for c in range(2):
            home = homes[chunk][c]
            if home == distance:

                @pl.when(g == 0)
                def _():
                    sum_copy(True, chunk, c, n).start()

            if home == last - distance:

                @pl.when(g == last)
                def _():
                    sum_copy(False, chunk, c, n).start()

    def sum_step(chunk, n, distance):
        for c in range(2):
            home = homes[chunk][c]
            if distance < home:

                @pl.when(g == distance)
                def _():
                    add_in(True, chunk, c, n)
                    sum_copy(True, chunk, c, n).start()

            if last - distance > home:

                @pl.when(g == last - distance)
                def _():
                    add_in(False, chunk, c, n)
                    sum_copy(False, chunk, c, n).start()

    def out_copies(n, local):
        side, start = divmod(n * span, feats)
        made = []
        for kind, ref in enumerate((out_main, out_tangent)):
            dst = ref.at[pl.ds(pl.multiple_of(x * half, half), half), pl.ds(start, span)]
            if local:
                made.append(pltpu.make_async_copy(fin.at[n, kind], dst, out_sem.at[n, kind]))
            else:
                made.append(remote(fin.at[n, kind], dst, out_send.at[n, kind], out_recv.at[n, kind], twin))
        return side, made

    def sum_final(chunk, n):
        for c in range(2):
            home = homes[chunk][c]

            @pl.when(g == home)
            def _():
                total = part[chunk, c, n].astype(jnp.float32)
                for way, needed in ((0, home > 0), (1, home < last)):
                    if needed:
                        sum_copy(way == 0, chunk, c, n).wait_recv()
                        total = total + arrived[way, chunk, c, n].astype(jnp.float32)
                for kind in range(2):
                    at = (kind * 2 + c) * half
                    for m in range(span // width):
                        s = (n * span % feats) // width + m
                        fin[n, kind, :, m * width : (m + 1) * width] = (
                            gat[chunk, s, n * span // feats, kind, c].astype(jnp.float32)
                            + total[kind, :, m * width : (m + 1) * width]
                        ).astype(jnp.bfloat16)
                side, local = out_copies(n, True)
                _, far = out_copies(n, False)

                @pl.when(x == side)
                def _():
                    for copy in local:
                        copy.start()

                @pl.when(x != side)
                def _():
                    for copy in far:
                        copy.start()

    sends = (2, 0, 1)
    w_in_first_pieces = ((2, 0), (2, 1), (0, 0), (1, 0))
    w_in_last_pieces = ((0, 1), (1, 1))
    inner = (g > 0) & (g < last)
    outer = (g == 0) | (g == last)

    def w_in_send(pieces):
        for r, p in pieces:
            wz_start(r, p).start()

    for j in range(8):
        for r in sends:
            z_start(r, j)

    @pl.when(inner)
    def _():
        w_in_send(w_in_first_pieces)

    locals_ = [pltpu.make_async_copy(piece(j, g), slot(j, g), own_sem.at[j]) for j in range(8)]
    for copy in locals_:
        copy.start()
    w_locals = [
        pltpu.make_async_copy(w_in_piece(g, p), w_in_slot(x, i, (g, p)), w_sem.at[p])
        for p in range(cuts)
    ] + [pltpu.make_async_copy(w_out, wol.at[x, i], w_sem.at[cuts])]
    for copy in w_locals:
        copy.start()
    for j in range(4):
        locals_[j].wait()
        kv_spread(3, j)
    for p in range(cuts):
        gi_start((g, p), (3, p), w_in_piece(g, p))
    for r in range(parts - 1):
        go_start(r, r, w_out_piece(r), (1,))

    def take(*which):
        for r, j in which:
            z_wait(r, j)
            kv_spread(r, j)

    def onward(*which):
        for r, j in which:
            kv_forward(r, j)

    def w_out_start(r):
        go_start(r, r, w_out_piece(r), (0, 2))

    take((2, 0), (0, 0))
    w_out_start(0)
    take((2, 1), (0, 1), (1, 0))
    onward((3, 0), (3, 1), (3, 2), (3, 3))
    for p in range(cuts):
        w_in_first(3, p)
    take((2, 2), (0, 2), (2, 3), (0, 3))
    w_out_start(1)
    for p in range(cuts):
        w_in_rest(3, p)
    onward((2, 0), (0, 0), (2, 1), (0, 1), (1, 0))
    go_first(0, 0)
    take((1, 1))
    w_out_start(2)
    onward((2, 2), (0, 2), (2, 3), (0, 3))
    w_out_rest(0)
    take((1, 2))
    onward((1, 1))
    go_first(1, 1)
    take((1, 3))
    go_first(2, 2)
    w_out_rest(1)
    onward((1, 2), (1, 3))
    w_out_rest(2)
    for j in range(4, 8):
        locals_[j].wait()
        for r in (2, 0, 1):
            z_wait(r, j)
        if j == 6:


            @pl.when(outer)
            def _():
                w_in_send(w_in_first_pieces)

    for j in range(4):
        for r in range(groups):
            kv_finish(r, j)
    attend_head(0, 0)
    w_in_start(2, 0)
    attend_head(0, 1)
    attend_head(0, 2)
    swap_start(0)
    line_step(0, 0, 0)
    w_in_start(2, 1)
    w_in_first(2, 0)
    attend_head(1, 0)
    w_in_start(1, 0)
    line_step(0, 1, 0)
    w_in_send(w_in_last_pieces)
    w_in_rest(2, 0)
    w_in_first(2, 1)
    attend_head(1, 1)
    w_in_rest(2, 1)
    w_in_first(1, 0)
    attend_head(1, 2)
    w_in_start(0, 0)
    line_step(0, 0, 1)
    w_in_rest(1, 0)
    w_in_first(0, 0)
    line_step(0, 1, 1)
    w_in_rest(0, 0)
    w_in_start(1, 1)
    w_in_start(0, 1)
    line_step(0, 0, 2)
    line_step(0, 1, 2)
    line_step(1, 0, 0)
    w_in_first(1, 1)
    w_in_first(0, 1)
    swap_start(1)
    w_in_rest(1, 1)
    go_start(3, 3, w_out_piece(3))
    w_in_rest(0, 1)
    line_step(1, 1, 0)
    line_step(1, 0, 1)
    for copy in w_locals:
        copy.wait()
    for p in range(cuts):
        for r in range(groups):
            gi_finish((ranks[r], p), (r, p))
    line_finish(0, 0)
    line_finish(0, 1)
    mine[0].wait()
    left = hidden_left(0)
    tiles = hid.shape[1] // HIDDEN_TILE
    for n in range(tiles):
        hidden_tile(left, n)
        if n == 0:
            line_step(1, 1, 1)
            go_first(3, 3)
        else:
            line_step(1, 0, 2)
    for r in range(parts - 1):
        go_finish(r, r)
    pairs = slices // 2
    order = [m for both in zip(range(pairs // 2), range(pairs // 2, pairs)) for m in both]
    order_n = [2 * m + n for m in order for n in range(2)]
    waiting = list(order_n)

    def sum_next(count):
        for n in waiting[:count]:
            sum_step(0, n, 1)
        del waiting[:count]

    for m in order:
        if m == order[1]:
            line_step(1, 1, 2)
        if m == order[-1]:
            w_out_rest(3)
            go_finish(3, 3)
        out_slices(0, m)
        for n in range(2):
            sum_start(0, 2 * m + n, 2)
        if m == order[1] or m == order[2]:
            sum_next(2)
    for n in order_n[:2]:
        sum_start(0, n, 1)
    for c in range(2):
        line_finish(1, c)
    mine[1].wait()
    left = hidden_left(1)
    sum_next(1)
    for n in range(tiles):
        hidden_tile(left, n)
        sum_next(1)
    for m in order:
        out_slices(1, m)
        for n in range(2):
            sum_start(1, 2 * m + n, 3)
        sum_next(1)
    for n in order_n[2:]:
        sum_start(0, n, 1)
    for at in range(slices + 2):
        if at < slices:
            sum_step(1, order_n[at], 1)
        if 0 < at <= slices:
            sum_step(1, order_n[at - 1], 2)
        if at > 1:
            sum_final(1, order_n[at - 2])
    for n in order_n:
        sum_final(0, n)
    for n in range(slices):
        side, local = out_copies(n, True)
        _, far = out_copies(n, False)

        @pl.when(x == side)
        def _():
            for copy in local:
                copy.wait()
            for copy in far:
                copy.wait_recv()

        @pl.when(x != side)
        def _():
            for copy in far:
                copy.wait_send()

    for copy in sent:
        copy.wait_send()
    for p in range(cuts):
        for r in range(last):
            wz_start(r, p).wait_send()
    for chunk in range(2):
        line_sent(chunk)
        for c in range(2):
            home = homes[chunk][c]
            for n in range(slices):

                @pl.when(g < home)
                def _():
                    sum_copy(True, chunk, c, n).wait_send()

                @pl.when(g > home)
                def _():
                    sum_copy(False, chunk, c, n).wait_send()


def deliver_kernel(main, tangent, out_main, out_tangent):
    out_main[...] = main[...]
    out_tangent[...] = tangent[...]


def deliver(main, tangent):
    return pl.pallas_call(
        deliver_kernel,
        in_specs=[pl.BlockSpec(memory_space=pltpu.VMEM)] * 2,
        out_specs=[pl.BlockSpec(memory_space=pltpu.VMEM)] * 2,
        out_shape=[jax.ShapeDtypeStruct(main.shape, main.dtype)] * 2,
        name="deliver",
    )(main, tangent)


SLICES = 8
PARTS = 4
CUTS = 2
HIDDEN_TILE = 896


def by_layers(query, key, value, d_query, d_key, d_value, residual, d_residual, w_in, w_out, dp, seq):
    groups = seq // INNER
    rows, feats = query.shape
    half, width = rows // dp, feats // groups
    deep, hidden = w_in.shape[0], w_in.shape[1] // groups
    whole = dp * feats
    span = whole // SLICES
    dma = pltpu.SemaphoreType.DMA
    low = jnp.bfloat16
    last = groups - 1
    length = groups * INNER * rows
    flops = 12 * groups * rows * length * width + 8 * dp * hidden * whole * groups * half * 2
    return tuple(deliver(*pl.pallas_call(
        block_kernel,
        in_specs=[pl.BlockSpec(memory_space=pl.ANY)] * 10,
        out_specs=[pl.BlockSpec(memory_space=pl.ANY)] * 2,
        out_shape=[jax.ShapeDtypeStruct((rows, feats), low)] * 2,
        scratch_shapes=[
            pltpu.VMEM((4, groups, rows, width), low),
            pltpu.VMEM((INNER, groups, 4, rows, width), low),
            pltpu.VMEM((groups, INNER, deep, dp * hidden), low),
            pltpu.VMEM((dp, INNER, w_out.shape[0], whole), low),
            pltpu.VMEM((dp, 2, 2, 2, half, width), low),
            pltpu.VMEM((2, groups, dp, 2, 2, half, width), low),
            pltpu.VMEM((4 * half, dp * hidden), low),
            pltpu.VMEM((2, 2, SLICES, 2, half, span), low),
            pltpu.VMEM((2, 2, 2, SLICES, 2, half, span), low),
            pltpu.VMEM((SLICES, 2, half, span), low),
            dma((last, 8)), dma((groups, 8)), dma((8,)),
        ]
        + [dma((groups, 4)) for _ in range(6)]
        + [dma((last, CUTS)), dma((groups, CUTS)), dma((groups, CUTS, 7)), dma((groups, CUTS, 7))]
        + [dma((PARTS, 7)), dma((PARTS, 7)), dma((CUTS + 1,))]
        + [dma((2,)), dma((2,)), dma((2,))]
        + [dma((2, 2, last)) for _ in range(4)]
        + [dma((2, 2, 2, SLICES)), dma((2, 2, 2, SLICES))]
        + [dma((SLICES, 2)) for _ in range(3)],
        cost_estimate=pl.CostEstimate(flops=flops, bytes_accessed=10**8, transcendentals=0),
        compiler_params=pltpu.CompilerParams(
            collective_id=0, has_side_effects=True, vmem_limit_bytes=60 * 2**20
        ),
        name="block",
    )(query, d_query, residual, d_residual, key, value, d_key, d_value, w_in, w_out)))


def on_device(*args, dp, seq):
    query, w_in = args[0], args[8]
    groups = seq // INNER
    tile = groups * HEAD_DIM
    if dp != 2 or seq % INNER or groups != 4 or query.shape[1] % tile or w_in.shape[1] % tile:
        return by_rows(*args)
    return by_layers(*args, dp=dp, seq=seq)


def solution(mesh):
    in_specs = (P("seq", "dp"),) * 9 + (P(("dp", "seq"), None),)
    out_specs = (P("seq", "dp"), P("seq", "dp"))
    body = functools.partial(on_device, dp=mesh.shape["dp"], seq=mesh.shape["seq"])
    return jax.shard_map(
        body, mesh=mesh, in_specs=in_specs, out_specs=out_specs, check_vma=False
    )
```
